768 devices in a mesh: batch: 128 (over y, x, z_hi, core), tm: 6 (over z_lo).
Axes of the slice: x: 4, y: 8, z: 12 (z_hi: 2, z_lo: 6; z = z_hi * 6 + z_lo), core: 2. Of those that a mesh axis runs over, the one named last changes fastest.
Arguments:
- audio: bfloat16 [512, 768, 768], P('batch', 'tm'), as said below
- video: bfloat16 [512, 128, 1024], P('batch'), as said below
- pair_ids: int32 [512], P('batch'), may hold values from 0 to 511, each once
- windows: int32 [512], P('batch'), may hold values from 1 to 32, as said below
- lengths: int32 [512], P('batch'), may hold values from 192 to 768, as said below
- w_qkv: bfloat16 [768, 2304], replicated, as said below
- w_out: bfloat16 [768, 768], replicated, may hold values from -0.21875 to 0.21875
- w_query: bfloat16 [1024, 768], replicated, may hold values from -0.1875 to 0.1875
- w_audio_embed: bfloat16 [768, 768], replicated, may hold values from -0.21875 to 0.21875
- w_video_embed: bfloat16 [768, 768], replicated, may hold values from -0.21875 to 0.21875
Outputs:
- audio_mixed: bfloat16 [512, 768, 768], P('batch', 'tm')
- audio_embed: float32 [512, 768], P('batch')
- video_embed: float32 [512, 768], P('batch')
- logits: float32 [512, 512], P('batch')
- row_loss: float32 [512], P('batch')
The draws below stay inside these ranges and needn't reach their ends.
Inputs may be any that keep to these rules, and one draw needn't show every extreme that they name: `pair_ids`: a permutation of the clip numbers. `windows`: some clip reaches 32 in every draw. `lengths`: some clip is valid over all 768 frames in every draw. `audio`: frame features. `video`: token features. `w_qkv`: projection weights of scale 768 to the minus one half.
All inputs are finite; a program needn't handle non-finite values.
Results may differ from the reference program's by a relative error of at most 0.0065.
Values may be sent and summed in bfloat16 or wider, within the bound.
A program may use at most 128 MiB of HBM per device.

```python
import jax
import jax.numpy as jnp
from jax import lax

HA = 12
HS = 64
DV = 1024
E = 768
FD = 128
VT = 128
DA = 768
WMAX = 32
CLIPS = 512
FRAMES = 768


def draw_audio(key, part):
    key_list = jax.random.split(key, 1)
    shape = (CLIPS, FRAMES, DA)
    return jax.random.normal(key_list[0], shape, jnp.float32).astype(jnp.bfloat16)


def draw_video(key, part):
    key_list = jax.random.split(key, 1)
    shape = (CLIPS, VT, DV)
    return jax.random.normal(key_list[0], shape, jnp.float32).astype(jnp.bfloat16)


def draw_w_qkv(key, part):
    key_list = jax.random.split(key, 3)
    factor = DA ** (-0.5)
    first_block = jax.random.normal(key_list[0], (DA, DA), jnp.float32) * factor
    second_block = jax.random.normal(key_list[1], (DA, DA), jnp.float32) * factor
    third_block = jax.random.normal(key_list[2], (DA, DA), jnp.float32) * factor
    return jnp.concatenate([first_block, second_block, third_block], axis=1).astype(jnp.bfloat16)


def draw_windows(key, part):
    key_one, key_two = jax.random.split(key, 2)
    drawn = jax.random.randint(key_one, (CLIPS,), 1, WMAX + 1)
    widest = jax.random.randint(key_two, (), 0, CLIPS)
    return jnp.where(jnp.arange(CLIPS, dtype=jnp.int32) == widest, WMAX, drawn).astype(jnp.int32)


def draw_lengths(key, part):
    key_one, key_two = jax.random.split(jax.random.fold_in(key, 7), 2)
    drawn = jax.random.randint(key_one, (CLIPS,), FRAMES // 4, FRAMES + 1)
    fullest = jax.random.randint(key_two, (), 0, CLIPS)
    return jnp.where(jnp.arange(CLIPS, dtype=jnp.int32) == fullest, FRAMES, drawn).astype(jnp.int32)


def bell_draw(key, shape, spread, bound, held_as=jnp.bfloat16):
    entries = jax.random.normal(key, shape, jnp.float32) * spread
    return jnp.minimum(jnp.maximum(entries, -bound), bound).astype(held_as)


def setup_inputs(seed: int = 0) -> dict:
    seeds = jax.random.split(jax.random.key(seed), 11)
    audio = draw_audio(jax.random.fold_in(seeds[10], 71), 0)
    video = draw_video(jax.random.fold_in(seeds[10], 71), 0)
    pair_ids = jax.random.permutation(seeds[2], CLIPS).astype(jnp.int32)
    windows = draw_windows(jax.random.fold_in(seeds[10], 71), 0)
    lengths = draw_lengths(jax.random.fold_in(seeds[10], 71), 0)
    w_qkv = draw_w_qkv(jax.random.fold_in(seeds[10], 71), 0)
    w_out = bell_draw(seeds[6], (DA, DA), DA ** -0.5, 0.21875)
    w_query = bell_draw(seeds[7], (DV, DA), DV ** -0.5, 0.1875)
    w_audio_embed = bell_draw(seeds[8], (DA, E), DA ** -0.5, 0.21875)
    w_video_embed = bell_draw(seeds[9], (DA, E), DA ** -0.5, 0.21875)
    return {"audio": audio, "video": video, "pair_ids": pair_ids, "windows": windows, "lengths": lengths, "w_qkv": w_qkv, "w_out": w_out, "w_query": w_query, "w_audio_embed": w_audio_embed, "w_video_embed": w_video_embed}


NEG_LARGE = -1e+30
LOGIT_SCALE = 10.0
LOGIT_BIAS = -10.0

def kept_bf16(array):
    return lax.optimization_barrier(array.astype(jnp.bfloat16)).astype(jnp.float32)

def softmax_parts(scores, allowed):
    scores = jnp.where(allowed, scores, NEG_LARGE)
    highest = lax.optimization_barrier(jnp.max(scores, axis=-1, keepdims=True))
    weights = jnp.where(allowed, jnp.exp(scores - highest), 0.0)
    return (weights, lax.optimization_barrier(jnp.sum(weights, axis=-1)))

def unit_rows(matrix):
    return matrix / jnp.sqrt(lax.optimization_barrier(jnp.sum(matrix * matrix, axis=1, keepdims=True)) + 1e-06)

def reference(audio, video, pair_ids, windows, lengths, w_qkv, w_out, w_query, w_audio_embed, w_video_embed):
    head_scale = HS ** (-0.5)
    blocks = FRAMES // FD
    key_span = FD + 2 * WMAX
    starts = jnp.arange(blocks, dtype=jnp.int32) * FD
    gather_index = starts[:, None] + jnp.arange(key_span, dtype=jnp.int32)[None, :]
    query_pos = starts[:, None] + jnp.arange(FD, dtype=jnp.int32)[None, :]
    key_pos = gather_index - WMAX
    distance = jnp.abs(query_pos[:, :, None] - key_pos[:, None, :])
    inside = ((key_pos >= 0) & (key_pos < FRAMES))[:, None, :]
    frame_index = jnp.arange(FRAMES, dtype=jnp.int32)

    def one_clip(packed):
        audio_clip, video_clip, window, length = packed
        projected = kept_bf16(jnp.dot(audio_clip, w_qkv, preferred_element_type=jnp.float32))
        queries = projected[:, :DA].reshape(blocks, FD, HA, HS)
        keys_all = projected[:, DA:2 * DA]
        values_all = projected[:, 2 * DA:]
        key_blocks = jnp.pad(keys_all, ((WMAX, WMAX), (0, 0)))[gather_index].reshape(blocks, key_span, HA, HS)
        value_blocks = jnp.pad(values_all, ((WMAX, WMAX), (0, 0)))[gather_index].reshape(blocks, key_span, HA, HS)
        allowed = (distance <= window) & inside & ((key_pos[:, None, :] < length) | (distance == 0))
        scores = jnp.einsum('bqhd,bkhd->bhqk', queries, key_blocks) * head_scale
        weights, totals = softmax_parts(scores, allowed[:, None])
        context = jnp.einsum('bhqk,bkhd->bqhd', kept_bf16(weights), value_blocks)
        context = context / jnp.transpose(totals, (0, 2, 1))[..., None]
        context = context.astype(jnp.bfloat16).reshape(FRAMES, DA)
        mixed_rows = (audio_clip.astype(jnp.float32) + jnp.dot(context, w_out, preferred_element_type=jnp.float32)).astype(jnp.bfloat16)
        asking = kept_bf16(jnp.dot(video_clip, w_query, preferred_element_type=jnp.float32)).reshape(VT, HA, HS)
        in_clip = frame_index < length
        cross_scores = jnp.einsum('qhd,khd->hqk', asking, keys_all.reshape(FRAMES, HA, HS)) * head_scale
        cross_weights, cross_totals = softmax_parts(cross_scores, in_clip[None, None, :])
        heard_ctx = jnp.einsum('hqk,khd->qhd', kept_bf16(cross_weights), values_all.reshape(FRAMES, HA, HS))
        heard_ctx = heard_ctx / jnp.transpose(cross_totals)[..., None]
        video_pool = lax.optimization_barrier(jnp.mean(heard_ctx, axis=0)).reshape(DA).astype(jnp.bfloat16)
        frame_sum = lax.optimization_barrier(jnp.sum(jnp.where(in_clip[:, None], mixed_rows.astype(jnp.float32), 0.0), axis=0))
        audio_pool = (frame_sum / length.astype(jnp.float32)).astype(jnp.bfloat16)
        return (mixed_rows, audio_pool, video_pool)
    audio_mixed, audio_pool, video_pool = lax.map(one_clip, (audio, video, windows, lengths))
    audio_embed = unit_rows(jnp.dot(audio_pool, w_audio_embed, preferred_element_type=jnp.float32))
    video_embed = unit_rows(jnp.dot(video_pool, w_video_embed, preferred_element_type=jnp.float32))
    logits = LOGIT_SCALE * jnp.dot(audio_embed, video_embed.T, precision=lax.Precision.HIGHEST) + LOGIT_BIAS
    columns = jnp.arange(CLIPS, dtype=jnp.int32)
    pair_signs = jnp.where(columns[None, :] == pair_ids[:, None], 1.0, -1.0)
    row_loss = lax.optimization_barrier(jnp.sum(jnp.logaddexp(0.0, -pair_signs * logits), axis=1))
    return (audio_mixed, audio_embed, video_embed, logits, row_loss)
```

```python
import jax
import jax.numpy as jnp
from jax import lax
from jax.experimental import pallas as pl
from jax.experimental.pallas import tpu as pltpu
from jax.sharding import PartitionSpec as P

NEG = -1e30
BF = jnp.bfloat16
F32 = jnp.float32
MESH = pl.DeviceIdType.MESH

CL = 4
FR = 128
D = 768
VT = 128
DV = 1024
PAIRS = 6
HALO = 32
EXT = FR + 2 * HALO
NX = 4
NZ = 2
NC = 2
NT = 6


def mm(a, b):
    return jnp.dot(a, b, preferred_element_type=F32)


def mmt(a, b):
    return lax.dot_general(a, b, (((1,), (1,)), ((), ())), preferred_element_type=F32)


def chunk(j, size):
    return pl.ds(pl.multiple_of(j * size, size), size)


def make_kernel(ny):
    clips_all = ny * NX * NZ * NC * CL

    def kernel(
        windows, lengths, pair_ids,
        audio_h, video_h, wqkv_h, wout_h, wask_h, wae_h, wve_h,
        mixed_o, ae_o, ve_o, logits_o, loss_o,
        audio_v, video_v, wq_v, wk_v, wv_v, wout_v, wask_v, wae_v, wve_v,
        hx, kx, vx, q_v, ask_v, o2_v, mt_v, lt_v, m_v, c_v, ctx_v, mixed_v,
        lse_all, fs_all, zp, gath, gp, ae_v, ve_v, lg_v,
        load_sem, out_sem, halo_s, halo_r, l_s, l_r, f_s, f_r, z_s, z_r,
        y_s, y_r, x_s, x_r, c_s, c_r,
    ):
        b = lax.axis_index("batch")
        t = lax.axis_index("tm")
        co = b % NC
        zh = (b // NC) % NZ
        x = (b // (NC * NZ)) % NX
        y = b // (NC * NZ * NX)
        z = zh * NT + t

        def batch_of(yy, xx, zz, cc):
            return ((yy * NX + xx) * NZ + zz) * NC + cc

        def load(src, dst, k):
            copy = pltpu.make_async_copy(src, dst, load_sem.at[k])
            copy.start()
            return copy

        ld_audio = load(audio_h, audio_v, 0)
        ld_k = load(wqkv_h.at[:, pl.ds(D, D)], wk_v, 1)
        ld_v = load(wqkv_h.at[:, pl.ds(2 * D, D)], wv_v, 2)
        ld_video = load(video_h, video_v, 3)
        ld_ask = load(wask_h, wask_v, 4)
        ld_q = load(wqkv_h.at[:, pl.ds(0, D)], wq_v, 5)
        ld_out = load(wout_h, wout_v, 6)
        ld_ve = load(wve_h, wve_v, 7)
        ld_ae = load(wae_h, wae_v, 8)

        def z_peer(k):
            zz = (z + k) % (NZ * NT)
            return (batch_of(y, x, zz // NT, co), zz % NT)

        def t_peer(k):
            return (b, (t + k) % NT)

        def y_peer(k):
            return (batch_of((y + k) % ny, x, zh, co), t)

        def x_peer(k):
            return (batch_of(y, (x + k) % NX, zh, co), t)

        core_peer = (batch_of(y, x, zh, 1 - co), t)

        peers = [z_peer(k) for k in range(1, NZ * NT)]
        peers += [y_peer(k) for k in range(1, ny)]
        peers += [x_peer(k) for k in range(1, NX)]
        peers += [core_peer]
        barrier = pltpu.get_barrier_semaphore()
        for peer in peers:
            pl.semaphore_signal(barrier, inc=1, device_id=peer, device_id_type=MESH)

        def remote(src, dst, s, r, peer):
            return pltpu.make_async_remote_copy(
                src_ref=src, dst_ref=dst, send_sem=s, recv_sem=r,
                device_id=peer, device_id_type=MESH,
            )

        ld_audio.wait()
        ld_k.wait()
        ld_v.wait()

        def kv_step(j, carry):
            cols = chunk(j, 256)
            rows = audio_v[...].reshape(CL * FR, D)
            kx[:, HALO:HALO + FR, cols] = mm(rows, wk_v[:, cols]).astype(BF).reshape(CL, FR, 256)
            vx[:, HALO:HALO + FR, cols] = mm(rows, wv_v[:, cols]).astype(BF).reshape(CL, FR, 256)
            return carry

        lax.fori_loop(0, 3, kv_step, 0)

        pl.semaphore_wait(barrier, len(peers))

        up = remote(
            audio_v.at[:, pl.ds(FR - HALO, HALO), :], hx.at[:, pl.ds(0, HALO), :],
            halo_s.at[0], halo_r.at[0], (b, jnp.minimum(t + 1, NT - 1)),
        )
        down = remote(
            audio_v.at[:, pl.ds(0, HALO), :], hx.at[:, pl.ds(HALO, HALO), :],
            halo_s.at[1], halo_r.at[1], (b, jnp.maximum(t - 1, 0)),
        )

        @pl.when(t < NT - 1)
        def _():
            up.start()

        @pl.when(t > 0)
        def _():
            down.start()

        @pl.when(t == 0)
        def _():
            hx[:, 0:HALO, :] = jnp.zeros((CL, HALO, D), BF)

        @pl.when(t == NT - 1)
        def _():
            hx[:, HALO:2 * HALO, :] = jnp.zeros((CL, HALO, D), BF)

        ld_video.wait()
        ld_ask.wait()

        def ask_step(j, carry):
            cols = chunk(j, 256)
            rows = video_v[...].reshape(CL * VT, DV)
            ask = mm(rows, wask_v[:, cols]).astype(BF) * jnp.asarray(0.125, BF)
            ask_v[:, :, cols] = ask.reshape(CL, VT, 256)
            return carry

        lax.fori_loop(0, 3, ask_step, 0)

        lane = lax.broadcasted_iota(jnp.int32, (128, 128), 1)
        low = lane < 64
        lane_row = lax.broadcasted_iota(jnp.int32, (1, 128), 1)
        ones = jnp.ones((128, 128), BF)
        zero_b = jnp.zeros((128, 128), BF)

        def cross_clip(c, carry):
            key_bias = jnp.where(t * FR + lane_row < lengths[c], 0.0, NEG)
            peak = jnp.zeros((128, 128), F32)
            total = jnp.zeros((128, 128), F32)
            for p in range(PAIRS):
                cols = slice(128 * p, 128 * p + 128)
                ask = ask_v[c, :, cols]
                ask2 = jnp.concatenate(
                    [jnp.where(low, ask, zero_b), jnp.where(low, zero_b, ask)], axis=0
                )
                keys = kx[c, HALO:HALO + FR, cols]
                values = vx[c, HALO:HALO + FR, cols]
                s = mmt(ask2, keys) + key_bias
                m = jnp.max(s, axis=1, keepdims=True)
                e = jnp.exp(s - m).astype(BF)
                o = mm(e, jnp.concatenate([values, ones], axis=1))
                for h in range(2):
                    rows = slice(128 * h, 128 * h + 128)
                    here = lane == (2 * p + h)
                    peak = jnp.where(here, m[rows], peak)
                    total = jnp.where(here, o[rows, 128:], total)
                    part = o[rows, :128].astype(BF)
                    o2_v[c * PAIRS + p, rows, :] = (
                        jnp.where(low, part, zero_b) if h == 0 else jnp.where(low, zero_b, part)
                    )
            mt_v[c] = peak
            lt_v[c] = total
            return carry

        lax.fori_loop(0, CL, cross_clip, 0)

        def table(ref):
            acc = ref[0]
            for c in range(1, CL):
                acc = acc + pltpu.roll(ref[c], 12 * c, 1)
            return jnp.transpose(acc)[0:48]

        peak48 = table(mt_v)
        m_v[...] = peak48
        lse_all[t] = peak48 + jnp.log(table(lt_v))

        l_copies = [
            remote(lse_all.at[t], lse_all.at[t], l_s.at[k], l_r.at[k], t_peer(k))
            for k in range(1, NT)
        ]
        for copy in l_copies:
            copy.start()

        ld_q.wait()

        def q_step(j, carry):
            cols = chunk(j, 256)
            rows = audio_v[...].reshape(CL * FR, D)
            q = mm(rows, wq_v[:, cols]).astype(BF) * jnp.asarray(0.125, BF)
            q_v[:, :, cols] = q.reshape(CL, FR, 256)
            return carry

        lax.fori_loop(0, 3, q_step, 0)

        @pl.when(t > 0)
        def _():
            up.wait_recv()

        @pl.when(t < NT - 1)
        def _():
            down.wait_recv()

        def halo_step(j, carry):
            cols = chunk(j, 256)
            rows = hx[...].reshape(CL * 2 * HALO, D)
            k = mm(rows, wk_v[:, cols]).astype(BF).reshape(CL, 2 * HALO, 256)
            kx[:, 0:HALO, cols] = k[:, :HALO]
            kx[:, HALO + FR:EXT, cols] = k[:, HALO:]
            v = mm(rows, wv_v[:, cols]).astype(BF).reshape(CL, 2 * HALO, 256)
            vx[:, 0:HALO, cols] = v[:, :HALO]
            vx[:, HALO + FR:EXT, cols] = v[:, HALO:]
            return carry

        lax.fori_loop(0, 3, halo_step, 0)
        ld_out.wait()

        row = lax.broadcasted_iota(jnp.int32, (128, 128), 0) % 64
        offset = row + HALO - lane
        distance = jnp.abs(offset)
        low64 = lane[:64] < 64
        zero_h = jnp.zeros((64, 128), BF)
        lane8 = lax.broadcasted_iota(jnp.int32, (8, 128), 1)

        def window_clip(c, carry):
            near = distance <= windows[c]
            length = lengths[c]
            for i in range(2):
                key_pos = lane + (t * FR + 64 * i - HALO)
                allowed = near & (key_pos >= 0) & ((key_pos < length) | (offset == 0))
                bias = jnp.where(allowed, 0.0, NEG)
                for p in range(PAIRS):
                    cols = slice(128 * p, 128 * p + 128)
                    q = q_v[c, 64 * i:64 * i + 64, cols]
                    q2 = jnp.concatenate(
                        [jnp.where(low64, q, zero_h), jnp.where(low64, zero_h, q)], axis=0
                    )
                    keys = kx[c, 64 * i:64 * i + 128, cols]
                    values = vx[c, 64 * i:64 * i + 128, cols]
                    s = mmt(q2, keys) + bias
                    m = jnp.max(s, axis=1, keepdims=True)
                    e = jnp.exp(s - m).astype(BF)
                    o = mm(e, jnp.concatenate([values, ones], axis=1))
                    top = jnp.where(low64, o[:64, :128], o[64:, :128])
                    bottom = jnp.where(low64, o[:64, 128:], o[64:, 128:])
                    ctx_v[64 * i:64 * i + 64, cols] = (top / bottom).astype(BF)
            in_clip = jnp.where(lane8 + t * FR < length, 1.0, 0.0).astype(BF)
            ctx = ctx_v[...]
            for j in range(3):
                cols = slice(256 * j, 256 * j + 256)
                mixed = mm(ctx, wout_v[:, cols]) + audio_v[c, :, cols].astype(F32)
                mixed = mixed.astype(BF)
                mixed_v[c, :, cols] = mixed
                fs_all[t, pl.ds(c, 1), cols] = mm(in_clip, mixed)[0:1]
            pltpu.make_async_copy(mixed_v.at[c], mixed_o.at[c], out_sem.at[c]).start()
            return carry

        lax.fori_loop(0, 2, window_clip, 0)

        for copy in l_copies:
            copy.wait()
        lse = lse_all[...]
        highest = jnp.max(lse, axis=0)
        whole = highest + jnp.log(jnp.sum(jnp.exp(lse - highest[None]), axis=0))
        c_v[...] = jnp.exp(m_v[...] - whole) * (1.0 / VT)
        for c in range(CL):
            for p in range(PAIRS):
                r = c * 12 + 2 * p
                pair = jnp.concatenate([c_v[r:r + 1], c_v[r + 1:r + 2]], axis=1).astype(BF)
                zp[z, c:c + 1, 128 * p:128 * p + 128] = mm(pair, o2_v[c * PAIRS + p])

        z_copies = [
            remote(zp.at[z], zp.at[z], z_s.at[k], z_r.at[k], z_peer(k))
            for k in range(1, NZ * NT)
        ]
        for copy in z_copies:
            copy.start()

        lax.fori_loop(2, CL, window_clip, 0)

        f_copies = [
            remote(fs_all.at[t], fs_all.at[t], f_s.at[k], f_r.at[k], t_peer(k))
            for k in range(1, NT)
        ]
        for copy in f_copies:
            copy.start()

        ld_ve.wait()
        for copy in z_copies:
            copy.wait()
        pools = jnp.concatenate(
            [jnp.sum(zp[0:NT], axis=0), jnp.sum(zp[NT:2 * NT], axis=0)], axis=0
        ).astype(BF)
        u = mm(pools, wve_v[...])
        embed = u / jnp.sqrt(jnp.sum(u * u, axis=1, keepdims=True) + 1e-06)
        gath[co, x, y] = embed.astype(BF)
        y_copies = [
            remote(gath.at[co, x, y], gath.at[co, x, y], y_s.at[k], y_r.at[k], y_peer(k))
            for k in range(1, ny)
        ]
        for copy in y_copies:
            copy.start()
        ve_v[...] = jnp.where(zh == 0, embed[:CL], embed[CL:])
        ve_out = pltpu.make_async_copy(ve_v, ve_o, out_sem.at[CL])
        ve_out.start()

        ld_ae.wait()
        for copy in f_copies:
            copy.wait()
        row4 = lax.broadcasted_iota(jnp.int32, (CL, 1), 0)
        count = jnp.zeros((CL, 1), F32)
        for c in range(CL):
            count = jnp.where(row4 == c, lengths[c].astype(F32), count)
        pool = jnp.sum(fs_all[...], axis=0) / count
        u = mm(jnp.concatenate([pool, pool], axis=0).astype(BF), wae_v[...])
        a_embed = u / jnp.sqrt(jnp.sum(u * u, axis=1, keepdims=True) + 1e-06)
        ae_v[...] = a_embed[:CL]
        ae_out = pltpu.make_async_copy(ae_v, ae_o, out_sem.at[CL + 1])
        ae_out.start()

        for copy in y_copies:
            copy.wait()
        x_copies = [
            remote(gath.at[co, x], gath.at[co, x], x_s.at[k], x_r.at[k], x_peer(k))
            for k in range(1, NX)
        ]
        for copy in x_copies:
            copy.start()
        c_copies = [
            remote(
                gath.at[co, (x + NX - k) % NX], gath.at[co, (x + NX - k) % NX],
                c_s.at[k], c_r.at[k], core_peer,
            )
            for k in range(NX)
        ]
        c_copies[0].start()
        for k in range(1, NX):
            x_copies[k - 1].wait()
            c_copies[k].start()
        for copy in c_copies:
            copy.wait()

        first = lax.broadcasted_iota(jnp.int32, (8, D), 0) < 4

        def order_rows(yy, carry):
            for xx in range(NX):
                one = gath[0, xx, yy].astype(F32)
                two = gath[1, xx, yy].astype(F32)
                top = jnp.where(first, one, pltpu.roll(two, 4, 0))
                bottom = jnp.where(first, pltpu.roll(one, 4, 0), two)
                gp[chunk(yy * NX + xx, 16), :] = jnp.concatenate([top, bottom], axis=0).astype(BF)
            return carry

        lax.fori_loop(0, ny, order_rows, 0)
        logits = mmt(a_embed.astype(BF), gp[...])[:CL] * 10.0 - 10.0
        lg_v[...] = logits
        lg_out = pltpu.make_async_copy(lg_v, logits_o, out_sem.at[CL + 2])
        lg_out.start()
        ids = jnp.zeros((CL, 1), jnp.int32)
        for c in range(CL):
            ids = jnp.where(row4 == c, pair_ids[c], ids)
        column = lax.broadcasted_iota(jnp.int32, (CL, clips_all), 1)
        signed = jnp.where(column == ids, -logits, logits)
        loss = jnp.maximum(signed, 0.0) + jnp.log1p(jnp.exp(-jnp.abs(signed)))
        for c in range(CL):
            loss_o[c] = jnp.sum(loss[c:c + 1])

        @pl.when(t < NT - 1)
        def _():
            up.wait_send()

        @pl.when(t > 0)
        def _():
            down.wait_send()

        for c in range(CL):
            pltpu.make_async_copy(mixed_v.at[c], mixed_o.at[c], out_sem.at[c]).wait()
        ve_out.wait()
        ae_out.wait()
        lg_out.wait()

    return kernel


def solution(mesh):
    nb = mesh.shape["batch"]
    ny = nb // (NX * NZ * NC)
    clips_all = nb * CL

    def per_device(
        audio, video, pair_ids, windows, lengths, w_qkv, w_out, w_query, w_audio_embed, w_video_embed
    ):
        smem = pl.BlockSpec(memory_space=pltpu.SMEM)
        hbm = pl.BlockSpec(memory_space=pl.ANY)
        dma = pltpu.SemaphoreType.DMA
        vm = pltpu.VMEM
        mixed, ae, ve, logits, loss = pl.pallas_call(
            make_kernel(ny),
            name="av_step",
            out_shape=(
                jax.ShapeDtypeStruct((CL, FR, D), BF),
                jax.ShapeDtypeStruct((CL, D), F32),
                jax.ShapeDtypeStruct((CL, D), F32),
                jax.ShapeDtypeStruct((CL, clips_all), F32),
                jax.ShapeDtypeStruct((CL,), F32),
            ),
            in_specs=[smem] * 3 + [hbm] * 7,
            out_specs=(hbm, hbm, hbm, hbm, smem),
            scratch_shapes=[
                vm((CL, FR, D), BF), vm((CL, VT, DV), BF),
                vm((D, D), BF), vm((D, D), BF), vm((D, D), BF), vm((D, D), BF),
                vm((DV, D), BF), vm((D, D), BF), vm((D, D), BF),
                vm((CL, 2 * HALO, D), BF), vm((CL, EXT, D), BF), vm((CL, EXT, D), BF),
                vm((CL, FR, D), BF), vm((CL, VT, D), BF), vm((CL * PAIRS, 256, 128), BF),
                vm((CL, 128, 128), F32), vm((CL, 128, 128), F32),
                vm((48, 128), F32), vm((48, 128), F32),
                vm((FR, D), BF), vm((CL, FR, D), BF),
                vm((NT, 48, 128), F32), vm((NT, CL, D), F32), vm((NZ * NT, CL, D), F32),
                vm((NC, NX, ny, 8, D), BF), vm((clips_all, D), BF),
                vm((CL, D), F32), vm((CL, D), F32), vm((CL, clips_all), F32),
                dma((9,)), dma((CL + 3,)), dma((2,)), dma((2,)),
                dma((NT,)), dma((NT,)), dma((NT,)), dma((NT,)),
                dma((NZ * NT,)), dma((NZ * NT,)),
                dma((ny,)), dma((ny,)), dma((NX,)), dma((NX,)), dma((NX,)), dma((NX,)),
            ],
            compiler_params=pltpu.CompilerParams(
                collective_id=0, has_side_effects=True, vmem_limit_bytes=56 * 1024 * 1024,
            ),
        )(windows, lengths, pair_ids, audio, video, w_qkv, w_out, w_query, w_audio_embed, w_video_embed)
        return mixed, ae, ve, logits, loss

    in_specs = (
        P("batch", "tm", None), P("batch", None, None), P("batch"), P("batch"), P("batch"),
        P(), P(), P(), P(), P(),
    )
    out_specs = (
        P("batch", "tm", None), P("batch", None), P("batch", None), P("batch", None), P("batch"),
    )
    return jax.shard_map(
        per_device, mesh=mesh, in_specs=in_specs, out_specs=out_specs, check_vma=False
    )
```

```python
import jax
import jax.numpy as jnp
from jax import lax
from jax.experimental import pallas as pl
from jax.experimental.pallas import tpu as pltpu
from jax.sharding import PartitionSpec as P

NEG = -1e30
BF = jnp.bfloat16
F32 = jnp.float32
MESH = pl.DeviceIdType.MESH

CL = 4
FR = 128
D = 768
VT = 128
DV = 1024
PAIRS = 6
HALO = 32
EXT = FR + 2 * HALO
NX = 4
NZ = 2
NC = 2
NT = 6


def mm(a, b):
    return jnp.dot(a, b, preferred_element_type=F32)


def mmt(a, b):
    return lax.dot_general(a, b, (((1,), (1,)), ((), ())), preferred_element_type=F32)


def chunk(j, size):
    return pl.ds(pl.multiple_of(j * size, size), size)


def make_kernel(ny):
    clips_all = ny * NX * NZ * NC * CL

    def kernel(
        windows, lengths, pair_ids,
        audio_h, video_h, wqkv_h, wout_h, wask_h, wae_h, wve_h,
        mixed_o, ae_o, ve_o, logits_o, loss_o,
        audio_v, video_v, wq_v, wk_v, wv_v, wout_v, wask_v, wae_v, wve_v,
        hx, kx, vx, q_v, ask_v, e_v, o2_v, mt_v, lt_v, m_v, c_v, ctx_v, mixed_v,
        lse_all, fs_all, zp, gath, gp, ae_v, ve_v, lg_v,
        load_sem, out_sem, halo_s, halo_r, l_s, l_r, f_s, f_r, z_s, z_r,
        y_s, y_r, x_s, x_r, c_s, c_r,
    ):
        b = lax.axis_index("batch")
        t = lax.axis_index("tm")
        co = b % NC
        zh = (b // NC) % NZ
        x = (b // (NC * NZ)) % NX
        y = b // (NC * NZ * NX)
        z = zh * NT + t

        def batch_of(yy, xx, zz, cc):
            return ((yy * NX + xx) * NZ + zz) * NC + cc

        def load(src, dst, k):
            return pltpu.make_async_copy(src, dst, load_sem.at[k])

        ld_audio = load(audio_h, audio_v, 0)
        ld_k = load(wqkv_h.at[:, pl.ds(D, D)], wk_v, 1)
        ld_v = load(wqkv_h.at[:, pl.ds(2 * D, D)], wv_v, 2)
        ld_video = load(video_h, video_v, 3)
        ld_ask = load(wask_h, wask_v, 4)
        ld_q = load(wqkv_h.at[:, pl.ds(0, D)], wq_v, 5)
        ld_out = load(wout_h, wout_v, 6)
        ld_ve = load(wve_h, wve_v, 7)
        ld_ae = load(wae_h, wae_v, 8)
        ld_audio.start()
        ld_k.start()
        ld_video.start()
        ld_ask.start()
        def z_peer(k):
            zz = (z + k) % (NZ * NT)
            return (batch_of(y, x, zz // NT, co), zz % NT)

        def t_peer(k):
            return (b, (t + k) % NT)

        def y_peer(k):
            return (batch_of((y + k) % ny, x, zh, co), t)

        def x_peer(k):
            return (batch_of(y, (x + k) % NX, zh, co), t)

        core_peer = (batch_of(y, x, zh, 1 - co), t)

        peers = [z_peer(k) for k in range(1, NZ * NT)]
        peers += [y_peer(k) for k in range(1, ny)]
        peers += [x_peer(k) for k in range(1, NX)]
        peers += [core_peer]
        barrier = pltpu.get_barrier_semaphore()
        for peer in peers:
            pl.semaphore_signal(barrier, inc=1, device_id=peer, device_id_type=MESH)

        def remote(src, dst, s, r, peer):
            return pltpu.make_async_remote_copy(
                src_ref=src, dst_ref=dst, send_sem=s, recv_sem=r,
                device_id=peer, device_id_type=MESH,
            )

        def project(j, weight, dst):
            cols = chunk(j, 256)
            rows = audio_v[...].reshape(CL * FR, D)
            dst[:, HALO:HALO + FR, cols] = mm(rows, weight[:, cols]).astype(BF).reshape(CL, FR, 256)

        def k_step(j, carry):
            project(j, wk_v, kx)
            return carry

        def v_step(j, carry):
            project(j, wv_v, vx)
            return carry

        def q_step(j, carry):
            cols = chunk(j, 256)
            rows = audio_v[...].reshape(CL * FR, D)
            q = mm(rows, wq_v[:, cols]).astype(BF) * jnp.asarray(0.125, BF)
            q_v[:, :, cols] = q.reshape(CL, FR, 256)
            return carry

        def ask_step(j, carry):
            cols = chunk(j, 256)
            rows = video_v[...].reshape(CL * VT, DV)
            ask = mm(rows, wask_v[:, cols]).astype(BF) * jnp.asarray(0.125, BF)
            ask_v[:, :, cols] = ask.reshape(CL, VT, 256)
            return carry

        ld_audio.wait()
        ld_k.wait()
        ld_v.start()
        lax.fori_loop(0, 3, k_step, 0)
        ld_video.wait()
        ld_ask.wait()
        ld_q.start()
        ld_out.start()
        lax.fori_loop(0, 3, ask_step, 0)

        pl.semaphore_wait(barrier, len(peers))

        up = remote(
            audio_v.at[:, pl.ds(FR - HALO, HALO), :], hx.at[:, pl.ds(0, HALO), :],
            halo_s.at[0], halo_r.at[0], (b, jnp.minimum(t + 1, NT - 1)),
        )
        down = remote(
            audio_v.at[:, pl.ds(0, HALO), :], hx.at[:, pl.ds(HALO, HALO), :],
            halo_s.at[1], halo_r.at[1], (b, jnp.maximum(t - 1, 0)),
        )

        @pl.when(t < NT - 1)
        def _():
            up.start()

        @pl.when(t > 0)
        def _():
            down.start()

        @pl.when(t == 0)
        def _():
            hx[:, 0:HALO, :] = jnp.zeros((CL, HALO, D), BF)

        @pl.when(t == NT - 1)
        def _():
            hx[:, HALO:2 * HALO, :] = jnp.zeros((CL, HALO, D), BF)

        lane = lax.broadcasted_iota(jnp.int32, (128, 128), 1)
        low = lane < 64
        lane_row = lax.broadcasted_iota(jnp.int32, (1, 128), 1)
        ones = jnp.ones((128, 128), BF)
        zero_b = jnp.zeros((128, 128), BF)

        def split_heads(block):
            return jnp.concatenate(
                [jnp.where(low, block, zero_b), jnp.where(low, zero_b, block)], axis=0
            )

        def cross_clip(c, carry):
            key_bias = jnp.where(t * FR + lane_row < lengths[c], 0.0, NEG)
            peak = jnp.zeros((128, 128), F32)
            total = jnp.zeros((128, 128), F32)
            for p in range(PAIRS):
                cols = slice(128 * p, 128 * p + 128)
                s = mmt(ask_v[c, :, cols], split_heads(kx[c, HALO:HALO + FR, cols]))
                here = (lane & 63) == p
                tops, sums = [], []
                for h in range(2):
                    part = s[:, 128 * h:128 * h + 128] + key_bias
                    m = jnp.max(part, axis=1, keepdims=True)
                    e = jnp.exp(part - m)
                    tops.append(m)
                    sums.append(jnp.sum(e, axis=1, keepdims=True))
                    e_v[c * PAIRS + p, :, 128 * h:128 * h + 128] = e.astype(BF)
                peak = jnp.where(here, jnp.where(low, tops[0], tops[1]), peak)
                total = jnp.where(here, jnp.where(low, sums[0], sums[1]), total)
            mt_v[c] = peak
            lt_v[c] = total
            return carry

        lax.fori_loop(0, CL, cross_clip, 0)

        def table(ref):
            acc = ref[0]
            for c in range(1, CL):
                acc = acc + pltpu.roll(ref[c], PAIRS * c, 1)
            flat = jnp.transpose(acc)
            return jnp.concatenate([flat[0:24], flat[64:88]], axis=0)

        peak48 = table(mt_v)
        m_v[...] = peak48
        lse_all[t] = peak48 + jnp.log(table(lt_v))

        l_copies = [
            remote(lse_all.at[t], lse_all.at[t], l_s.at[k], l_r.at[k], t_peer(k))
            for k in range(1, NT)
        ]
        for copy in l_copies:
            copy.start()

        ld_v.wait()
        ld_ve.start()
        ld_ae.start()
        lax.fori_loop(0, 3, v_step, 0)

        def hear_clip(c, carry):
            for p in range(PAIRS):
                cols = slice(128 * p, 128 * p + 128)
                heard = mm(e_v[c * PAIRS + p], split_heads(vx[c, HALO:HALO + FR, cols]))
                o2_v[c * PAIRS + p] = heard.astype(BF)
            return carry

        lax.fori_loop(0, CL, hear_clip, 0)

        ld_q.wait()
        lax.fori_loop(0, 3, q_step, 0)

        @pl.when(t > 0)
        def _():
            up.wait_recv()

        @pl.when(t < NT - 1)
        def _():
            down.wait_recv()

        def halo_step(j, carry):
            cols = chunk(j, 256)
            rows = hx[...].reshape(CL * 2 * HALO, D)
            k = mm(rows, wk_v[:, cols]).astype(BF).reshape(CL, 2 * HALO, 256)
            kx[:, 0:HALO, cols] = k[:, :HALO]
            kx[:, HALO + FR:EXT, cols] = k[:, HALO:]
            v = mm(rows, wv_v[:, cols]).astype(BF).reshape(CL, 2 * HALO, 256)
            vx[:, 0:HALO, cols] = v[:, :HALO]
            vx[:, HALO + FR:EXT, cols] = v[:, HALO:]
            return carry

        lax.fori_loop(0, 3, halo_step, 0)

        for copy in l_copies:
            copy.wait()
        lse = lse_all[...]
        highest = jnp.max(lse, axis=0)
        whole = highest + jnp.log(jnp.sum(jnp.exp(lse - highest[None]), axis=0))
        c_v[...] = jnp.exp(m_v[...] - whole) * (1.0 / VT)
        for c in range(CL):
            for p in range(PAIRS):
                r = c * PAIRS + p
                pair = jnp.concatenate([c_v[r:r + 1], c_v[24 + r:25 + r]], axis=0).astype(BF)
                both = mm(pair, o2_v[r])
                zp[z, c:c + 1, 128 * p:128 * p + 128] = jnp.where(
                    lane_row < 64, both[0:1], both[1:2]
                )

        z_copies = [
            remote(zp.at[z], zp.at[z], z_s.at[k], z_r.at[k], z_peer(k))
            for k in range(1, NZ * NT)
        ]
        for copy in z_copies:
            copy.start()

        row64 = lax.broadcasted_iota(jnp.int32, (64, 128), 0)
        lane64 = lax.broadcasted_iota(jnp.int32, (64, 128), 1)
        offset = row64 + HALO - lane64
        distance = jnp.abs(offset)
        low64 = lane64 < 64

        def window_clip(c, carry):
            near = distance <= windows[c]
            length = lengths[c]
            for i in range(2):
                key_pos = lane64 + (t * FR + 64 * i - HALO)
                allowed = near & (key_pos >= 0) & ((key_pos < length) | (offset == 0))
                bias = jnp.where(allowed, 0.0, NEG)
                for p in range(PAIRS):
                    cols = slice(128 * p, 128 * p + 128)
                    keys = split_heads(kx[c, 64 * i:64 * i + 128, cols])
                    s = mmt(q_v[c, 64 * i:64 * i + 64, cols], keys)
                    es = []
                    for h in range(2):
                        part = s[:, 128 * h:128 * h + 128] + bias
                        m = jnp.max(part, axis=1, keepdims=True)
                        es.append(jnp.exp(part - m).astype(BF))
                    e = jnp.concatenate(es, axis=0)
                    values = vx[c, 64 * i:64 * i + 128, cols]
                    o = mm(e, jnp.concatenate([values, ones], axis=1))
                    top = jnp.where(low64, o[:64, :128], o[64:, :128])
                    bottom = jnp.where(low64, o[:64, 128:], o[64:, 128:])
                    ctx_v[c, 64 * i:64 * i + 64, cols] = (top / bottom).astype(BF)
            return carry

        lax.fori_loop(0, CL, window_clip, 0)

        ld_out.wait()
        frame = lax.broadcasted_iota(jnp.int32, (FR, 1), 0) + t * FR

        def out_step(j, carry):
            cols = chunk(j, 256)
            rows = ctx_v[...].reshape(CL * FR, D)
            mixed = mm(rows, wout_v[:, cols]).reshape(CL, FR, 256) + audio_v[:, :, cols].astype(F32)
            mixed = mixed.astype(BF)
            mixed_v[:, :, cols] = mixed
            wide = mixed.astype(F32)
            for c in range(CL):
                kept = jnp.where(frame < lengths[c], wide[c], 0.0)
                fs_all[t, c:c + 1, cols] = jnp.sum(kept, axis=0, keepdims=True)
            return carry

        lax.fori_loop(0, 3, out_step, 0)
        mixed_out = pltpu.make_async_copy(mixed_v, mixed_o, out_sem.at[0])
        mixed_out.start()

        f_copies = [
            remote(fs_all.at[t], fs_all.at[t], f_s.at[k], f_r.at[k], t_peer(k))
            for k in range(1, NT)
        ]
        for copy in f_copies:
            copy.start()

        ld_ve.wait()
        for copy in z_copies:
            copy.wait()
        pools = jnp.concatenate(
            [jnp.sum(zp[0:NT], axis=0), jnp.sum(zp[NT:2 * NT], axis=0)], axis=0
        ).astype(BF)
        u = mm(pools, wve_v[...])
        embed = u / jnp.sqrt(jnp.sum(u * u, axis=1, keepdims=True) + 1e-06)
        gath[co, x, y] = embed.astype(BF)
        around = [0]
        for k in range(1, ny // 2 + 1):
            around += [k] if 2 * k == ny else [k, ny - k]
        y_copies = {
            k: remote(gath.at[co, x, y], gath.at[co, x, y], y_s.at[k], y_r.at[k], y_peer(k))
            for k in around[1:]
        }

        step = 1 - 2 * co
        behind = (x + NX - step) % NX
        x_copies, c_copies = {}, []

        def to_core(k, n, xx):
            yy = (y + ny - k) % ny
            copy = remote(
                gath.at[co, xx, yy], gath.at[co, xx, yy],
                c_s.at[k, n], c_r.at[k, n], core_peer,
            )
            copy.start()
            c_copies.append(copy)

        def along_x(k):
            yy = (y + ny - k) % ny
            block = gath.at[co, x, yy]
            ahead = gath.at[co, behind, yy]
            x_copies[k] = [
                remote(block, block, x_s.at[k, 0], x_r.at[k, 0], x_peer(1)),
                remote(block, block, x_s.at[k, 1], x_r.at[k, 1], x_peer(NX - 1)),
                remote(ahead, ahead, x_s.at[k, 2], x_r.at[k, 2], (batch_of(y, (x + NX + step) % NX, zh, co), t)),
            ]
            x_copies[k][0].start()
            x_copies[k][1].start()
            to_core(k, 0, x)

        def pass_on(k):
            x_copies[k][0].wait_recv()
            x_copies[k][1].wait_recv()
            x_copies[k][2].start()
            to_core(k, 1, (x + NX - 1) % NX)
            to_core(k, 2, (x + 1) % NX)

        def last_x(k):
            x_copies[k][2].wait_recv()
            to_core(k, 3, (x + 2) % NX)

        for k in around[1:]:
            y_copies[k].start()
        along_x(0)
        ve_v[...] = jnp.where(zh == 0, embed[:CL], embed[CL:])
        ve_out = pltpu.make_async_copy(ve_v, ve_o, out_sem.at[1])
        ve_out.start()

        ld_ae.wait()
        for copy in f_copies:
            copy.wait()
        row4 = lax.broadcasted_iota(jnp.int32, (CL, 1), 0)
        count = jnp.zeros((CL, 1), F32)
        for c in range(CL):
            count = jnp.where(row4 == c, lengths[c].astype(F32), count)
        pool = jnp.sum(fs_all[...], axis=0) / count
        u = mm(jnp.concatenate([pool, pool], axis=0).astype(BF), wae_v[...])
        a_embed = u / jnp.sqrt(jnp.sum(u * u, axis=1, keepdims=True) + 1e-06)
        ae_v[...] = a_embed[:CL]
        ae_out = pltpu.make_async_copy(ae_v, ae_o, out_sem.at[2])
        ae_out.start()

        rounds = [around[0:1]] + [around[i:i + 2] for i in range(1, ny, 2)]
        for n in range(len(rounds) + 2):
            if 0 < n < len(rounds):
                for k in rounds[n]:
                    y_copies[k].wait_recv()
                    along_x(k)
            if 0 <= n - 1 < len(rounds):
                for k in rounds[n - 1]:
                    pass_on(k)
            if 0 <= n - 2 < len(rounds):
                for k in rounds[n - 2]:
                    last_x(k)
        for copy in c_copies:
            copy.wait()

        first = lax.broadcasted_iota(jnp.int32, (8, D), 0) < 4

        def order_rows(yy, carry):
            for xx in range(NX):
                one = gath[0, xx, yy].astype(F32)
                two = gath[1, xx, yy].astype(F32)
                top = jnp.where(first, one, pltpu.roll(two, 4, 0))
                bottom = jnp.where(first, pltpu.roll(one, 4, 0), two)
                gp[chunk(yy * NX + xx, 16), :] = jnp.concatenate([top, bottom], axis=0).astype(BF)
            return carry

        lax.fori_loop(0, ny, order_rows, 0)
        logits = mmt(a_embed.astype(BF), gp[...])[:CL] * 10.0 - 10.0
        lg_v[...] = logits
        lg_out = pltpu.make_async_copy(lg_v, logits_o, out_sem.at[3])
        lg_out.start()
        ids = jnp.zeros((CL, 1), jnp.int32)
        for c in range(CL):
            ids = jnp.where(row4 == c, pair_ids[c], ids)
        column = lax.broadcasted_iota(jnp.int32, (CL, clips_all), 1)
        signed = jnp.where(column == ids, -logits, logits)
        loss = jnp.maximum(signed, 0.0) + jnp.log1p(jnp.exp(-jnp.abs(signed)))
        for c in range(CL):
            loss_o[c] = jnp.sum(loss[c:c + 1])

        @pl.when(t < NT - 1)
        def _():
            up.wait_send()

        @pl.when(t > 0)
        def _():
            down.wait_send()

        for k in around[1:]:
            y_copies[k].wait_send()
        for k in around:
            for copy in x_copies[k]:
                copy.wait_send()
        mixed_out.wait()
        ve_out.wait()
        ae_out.wait()
        lg_out.wait()

    return kernel


def solution(mesh):
    nb = mesh.shape["batch"]
    ny = nb // (NX * NZ * NC)
    clips_all = nb * CL

    def per_device(
        audio, video, pair_ids, windows, lengths, w_qkv, w_out, w_query, w_audio_embed, w_video_embed
    ):
        smem = pl.BlockSpec(memory_space=pltpu.SMEM)
        hbm = pl.BlockSpec(memory_space=pl.ANY)
        dma = pltpu.SemaphoreType.DMA
        vm = pltpu.VMEM
        mixed, ae, ve, logits, loss = pl.pallas_call(
            make_kernel(ny),
            name="av_step",
            out_shape=(
                jax.ShapeDtypeStruct((CL, FR, D), BF),
                jax.ShapeDtypeStruct((CL, D), F32),
                jax.ShapeDtypeStruct((CL, D), F32),
                jax.ShapeDtypeStruct((CL, clips_all), F32),
                jax.ShapeDtypeStruct((CL,), F32),
            ),
            in_specs=[smem] * 3 + [hbm] * 7,
            out_specs=(hbm, hbm, hbm, hbm, smem),
            scratch_shapes=[
                vm((CL, FR, D), BF), vm((CL, VT, DV), BF),
                vm((D, D), BF), vm((D, D), BF), vm((D, D), BF), vm((D, D), BF),
                vm((DV, D), BF), vm((D, D), BF), vm((D, D), BF),
                vm((CL, 2 * HALO, D), BF), vm((CL, EXT, D), BF), vm((CL, EXT, D), BF),
                vm((CL, FR, D), BF), vm((CL, VT, D), BF), vm((CL * PAIRS, VT, 256), BF), vm((CL * PAIRS, VT, 128), BF),
                vm((CL, 128, 128), F32), vm((CL, 128, 128), F32),
                vm((48, 128), F32), vm((48, 128), F32),
                vm((CL, FR, D), BF), vm((CL, FR, D), BF),
                vm((NT, 48, 128), F32), vm((NT, CL, D), F32), vm((NZ * NT, CL, D), F32),
                vm((NC, NX, ny, 8, D), BF), vm((clips_all, D), BF),
                vm((CL, D), F32), vm((CL, D), F32), vm((CL, clips_all), F32),
                dma((9,)), dma((4,)), dma((2,)), dma((2,)),
                dma((NT,)), dma((NT,)), dma((NT,)), dma((NT,)),
                dma((NZ * NT,)), dma((NZ * NT,)),
                dma((ny,)), dma((ny,)), dma((ny, 3)), dma((ny, 3)), dma((ny, NX)), dma((ny, NX)),
            ],
            compiler_params=pltpu.CompilerParams(
                collective_id=0, has_side_effects=True, vmem_limit_bytes=56 * 1024 * 1024,
            ),
        )(windows, lengths, pair_ids, audio, video, w_qkv, w_out, w_query, w_audio_embed, w_video_embed)
        return mixed, ae, ve, logits, loss

    in_specs = (
        P("batch", "tm", None), P("batch", None, None), P("batch"), P("batch"), P("batch"),
        P(), P(), P(), P(), P(),
    )
    out_specs = (
        P("batch", "tm", None), P("batch", None), P("batch", None), P("batch", None), P("batch"),
    )
    return jax.shard_map(
        per_device, mesh=mesh, in_specs=in_specs, out_specs=out_specs, check_vma=False
    )
```

```python
import jax
import jax.numpy as jnp
from jax import lax
from jax.experimental import pallas as pl
from jax.experimental.pallas import tpu as pltpu
from jax.sharding import PartitionSpec as P

NEG = -1e30
BF = jnp.bfloat16
F32 = jnp.float32
MESH = pl.DeviceIdType.MESH

CL = 4
FR = 128
D = 768
VT = 128
DV = 1024
PAIRS = 6
HALO = 32
EXT = FR + 2 * HALO
NX = 4
NZ = 2
NC = 2
NT = 6


def mm(a, b):
    return jnp.dot(a, b, preferred_element_type=F32)


def mmt(a, b):
    return lax.dot_general(a, b, (((1,), (1,)), ((), ())), preferred_element_type=F32)


def chunk(j, size):
    return pl.ds(pl.multiple_of(j * size, size), size)


def write_out(mixed_v, ae_v, ve_v, lg_v, loss_v, mixed_o, ae_o, ve_o, lg_o, loss_o, sem):
    copies = [
        pltpu.make_async_copy(src, dst, sem.at[k])
        for k, (src, dst) in enumerate(
            ((mixed_v, mixed_o), (ae_v, ae_o), (ve_v, ve_o), (lg_v, lg_o))
        )
    ]
    for copy in copies:
        copy.start()
    for c in range(CL):
        loss_o[c] = jnp.max(loss_v[c:c + 1, :])
    for copy in copies:
        copy.wait()


def make_kernel(ny):
    clips_all = ny * NX * NZ * NC * CL

    def kernel(
        windows, lengths, pair_ids,
        audio_h, video_h, wqkv_h, wout_h, wask_h, wae_h, wve_h,
        mixed_v, ae_v, ve_v, lg_v, loss_v,
        audio_v, video_v, wq_v, wk_v, wv_v, wout_v, wask_v, wae_v, wve_v,
        hx, kx, vx, q_v, ask_v, e_v, o2_v, mt_v, lt_v, m_v, c_v, ctx_v,
        lse_all, fs_all, share, zp, gath, gp,
        load_sem, halo_s, halo_r, l_s, l_r, f_s, f_r, z_s, z_r,
        y_s, y_r, x_s, x_r, c_s, c_r,
    ):
        b = lax.axis_index("batch")
        t = lax.axis_index("tm")
        co = b % NC
        zh = (b // NC) % NZ
        x = (b // (NC * NZ)) % NX
        y = b // (NC * NZ * NX)
        z = zh * NT + t

        def batch_of(yy, xx, zz, cc):
            return ((yy * NX + xx) * NZ + zz) * NC + cc

        def load(src, dst, k):
            return pltpu.make_async_copy(src, dst, load_sem.at[k])

        ld_audio = load(audio_h, audio_v, 0)
        ld_k = load(wqkv_h.at[:, pl.ds(D, D)], wk_v, 1)
        ld_v = load(wqkv_h.at[:, pl.ds(2 * D, D)], wv_v, 2)
        ld_video = load(video_h, video_v, 3)
        ld_ask = load(wask_h, wask_v, 4)
        ld_q = load(wqkv_h.at[:, pl.ds(0, D)], wq_v, 5)
        ld_out = load(wout_h, wout_v, 6)
        ld_ve = load(wve_h, wve_v, 7)
        ld_ae = load(wae_h, wae_v, 8)
        for copy in (ld_audio, ld_k, ld_video, ld_ask):
            copy.start()
        def z_peer(k):
            zz = (z + k) % (NZ * NT)
            return (batch_of(y, x, zz // NT, co), zz % NT)

        def t_peer(k):
            return (b, (t + k) % NT)

        def y_peer(k):
            return (batch_of((y + k) % ny, x, zh, co), t)

        def x_peer(k):
            return (batch_of(y, (x + k) % NX, zh, co), t)

        core_peer = (batch_of(y, x, zh, 1 - co), t)

        peers = [z_peer(k) for k in range(1, NZ * NT)]
        peers += [y_peer(k) for k in range(1, ny)]
        peers += [x_peer(k) for k in range(1, NX)]
        peers += [core_peer]
        barrier = pltpu.get_barrier_semaphore()
        for peer in peers:
            pl.semaphore_signal(barrier, inc=1, device_id=peer, device_id_type=MESH)

        def remote(src, dst, s, r, peer):
            return pltpu.make_async_remote_copy(
                src_ref=src, dst_ref=dst, send_sem=s, recv_sem=r,
                device_id=peer, device_id_type=MESH,
            )

        def project(j, weight, dst):
            cols = chunk(j, 256)
            rows = audio_v[...].reshape(CL * FR, D)
            dst[:, HALO:HALO + FR, cols] = mm(rows, weight[:, cols]).astype(BF).reshape(CL, FR, 256)

        def k_step(j, carry):
            project(j, wk_v, kx)
            return carry

        def v_step(j, carry):
            project(j, wv_v, vx)
            return carry

        def q_step(j, carry):
            cols = chunk(j, 256)
            rows = audio_v[...].reshape(CL * FR, D)
            q = mm(rows, wq_v[:, cols]).astype(BF) * jnp.asarray(0.125, BF)
            q_v[:, :, cols] = q.reshape(CL, FR, 256)
            return carry

        def ask_step(j, carry):
            cols = chunk(j, 256)
            rows = video_v[...].reshape(CL * VT, DV)
            ask = mm(rows, wask_v[:, cols]).astype(BF) * jnp.asarray(0.125, BF)
            ask_v[:, :, cols] = ask.reshape(CL, VT, 256)
            return carry

        ld_audio.wait()
        ld_k.wait()
        lax.fori_loop(0, 3, k_step, 0)
        ld_video.wait()
        ld_ask.wait()
        for copy in (ld_v, ld_q, ld_ve, ld_out, ld_ae):
            copy.start()
        lax.fori_loop(0, 3, ask_step, 0)

        pl.semaphore_wait(barrier, len(peers))

        up = remote(
            audio_v.at[:, pl.ds(FR - HALO, HALO), :], hx.at[:, pl.ds(0, HALO), :],
            halo_s.at[0], halo_r.at[0], (b, jnp.minimum(t + 1, NT - 1)),
        )
        down = remote(
            audio_v.at[:, pl.ds(0, HALO), :], hx.at[:, pl.ds(HALO, HALO), :],
            halo_s.at[1], halo_r.at[1], (b, jnp.maximum(t - 1, 0)),
        )

        @pl.when(t < NT - 1)
        def _():
            up.start()

        @pl.when(t > 0)
        def _():
            down.start()

        @pl.when(t == 0)
        def _():
            hx[:, 0:HALO, :] = jnp.zeros((CL, HALO, D), BF)

        @pl.when(t == NT - 1)
        def _():
            hx[:, HALO:2 * HALO, :] = jnp.zeros((CL, HALO, D), BF)

        lane = lax.broadcasted_iota(jnp.int32, (128, 128), 1)
        low = lane < 64
        lane_row = lax.broadcasted_iota(jnp.int32, (1, 128), 1)
        zero_b = jnp.zeros((128, 128), BF)

        def split_heads(block):
            return jnp.concatenate(
                [jnp.where(low, block, zero_b), jnp.where(low, zero_b, block)], axis=0
            )

        marks = jnp.concatenate(
            [jnp.where(low, 1.0, 0.0), jnp.where(low, 0.0, 1.0)], axis=0
        ).astype(BF)

        def cross_clip(c, carry):
            key_bias = jnp.where(t * FR + lane_row < lengths[c], 0.0, NEG)
            peak = jnp.zeros((128, 128), F32)
            total = jnp.zeros((128, 128), F32)
            pairs = [slice(128 * p, 128 * p + 128) for p in range(PAIRS)]
            scores = [
                mmt(ask_v[c, :, cols], split_heads(kx[c, HALO:HALO + FR, cols])) for cols in pairs
            ]
            for p in range(PAIRS):
                here = (lane & 63) == p
                tops, es = [], []
                for h in range(2):
                    part = scores[p][:, 128 * h:128 * h + 128] + key_bias
                    m = jnp.max(part, axis=1, keepdims=True)
                    tops.append(m)
                    es.append(jnp.exp(part - m).astype(BF))
                e = jnp.concatenate(es, axis=1)
                e_v[c * PAIRS + p] = e
                peak = jnp.where(here, jnp.where(low, tops[0], tops[1]), peak)
                total = jnp.where(here, mm(e, marks), total)
            mt_v[c] = peak
            lt_v[c] = total
            return carry

        lax.fori_loop(0, CL, cross_clip, 0)

        def table(ref):
            acc = ref[0]
            for c in range(1, CL):
                acc = acc + pltpu.roll(ref[c], PAIRS * c, 1)
            flat = jnp.transpose(acc)
            return jnp.concatenate([flat[0:24], flat[64:88]], axis=0)

        peak48 = table(mt_v)
        m_v[...] = peak48
        lse_all[t] = peak48 + jnp.log(table(lt_v))

        l_copies = [
            remote(lse_all.at[t], lse_all.at[t], l_s.at[k], l_r.at[k], t_peer(k))
            for k in range(1, NT)
        ]
        for copy in l_copies:
            copy.start()

        ld_v.wait()
        lax.fori_loop(0, 3, v_step, 0)

        def hear_clip(c, carry):
            for p in range(PAIRS):
                cols = slice(128 * p, 128 * p + 128)
                heard = mm(e_v[c * PAIRS + p], split_heads(vx[c, HALO:HALO + FR, cols]))
                o2_v[c * PAIRS + p] = heard.astype(BF)
            return carry

        lax.fori_loop(0, CL, hear_clip, 0)

        ld_q.wait()
        lax.fori_loop(0, 3, q_step, 0)

        @pl.when(t > 0)
        def _():
            up.wait_recv()

        @pl.when(t < NT - 1)
        def _():
            down.wait_recv()

        def halo_step(j, carry):
            cols = chunk(j, 256)
            rows = hx[...].reshape(CL * 2 * HALO, D)
            k = mm(rows, wk_v[:, cols]).astype(BF).reshape(CL, 2 * HALO, 256)
            kx[:, 0:HALO, cols] = k[:, :HALO]
            kx[:, HALO + FR:EXT, cols] = k[:, HALO:]
            v = mm(rows, wv_v[:, cols]).astype(BF).reshape(CL, 2 * HALO, 256)
            vx[:, 0:HALO, cols] = v[:, :HALO]
            vx[:, HALO + FR:EXT, cols] = v[:, HALO:]
            return carry

        lax.fori_loop(0, 3, halo_step, 0)

        for copy in l_copies:
            copy.wait()
        lse = lse_all[...]
        highest = jnp.max(lse, axis=0)
        whole = highest + jnp.log(jnp.sum(jnp.exp(lse - highest[None]), axis=0))
        c_v[...] = jnp.exp(m_v[...] - whole) * (1.0 / VT)
        for c in range(CL):
            for p in range(PAIRS):
                r = c * PAIRS + p
                pair = jnp.concatenate([c_v[r:r + 1], c_v[24 + r:25 + r]], axis=0).astype(BF)
                both = mm(pair, o2_v[r])
                share[c:c + 1, 128 * p:128 * p + 128] = jnp.where(
                    lane_row < 64, both[0:1], both[1:2]
                )

        zp[z] = share[...].astype(BF)
        z_copies = [
            remote(zp.at[z], zp.at[z], z_s.at[k], z_r.at[k], z_peer(k))
            for k in range(1, NZ * NT)
        ]
        for copy in z_copies:
            copy.start()

        row64 = lax.broadcasted_iota(jnp.int32, (64, 128), 0)
        lane64 = lax.broadcasted_iota(jnp.int32, (64, 128), 1)
        offset = row64 + HALO - lane64
        distance = jnp.abs(offset)

        def window_clip(c, carry):
            near = distance <= windows[c]
            length = lengths[c]
            biases = []
            for i in range(2):
                key_pos = lane64 + (t * FR + 64 * i - HALO)
                allowed = near & (key_pos >= 0) & ((key_pos < length) | (offset == 0))
                biases.append(jnp.where(allowed, 0.0, NEG))
            blocks = [
                (i, slice(64 * i, 64 * i + 64), slice(64 * i, 64 * i + 128), slice(128 * p, 128 * p + 128))
                for i in range(2) for p in range(PAIRS)
            ]
            scores = [
                mmt(q_v[c, rows, cols], split_heads(kx[c, keys, cols])) for _, rows, keys, cols in blocks
            ]
            weights = []
            for (i, _, _, _), s in zip(blocks, scores):
                es = []
                for h in range(2):
                    part = s[:, 128 * h:128 * h + 128] + biases[i]
                    m = jnp.max(part, axis=1, keepdims=True)
                    es.append(jnp.exp(part - m).astype(BF))
                weights.append(jnp.concatenate(es, axis=1))
            for (_, rows, keys, cols), e in zip(blocks, weights):
                values = split_heads(vx[c, keys, cols])
                o = mm(e, jnp.concatenate([values, marks], axis=1))
                ctx_v[c, rows, cols] = (o[:, :128] / o[:, 128:]).astype(BF)
            return carry

        lax.fori_loop(0, CL, window_clip, 0)

        ld_out.wait()
        frame = lax.broadcasted_iota(jnp.int32, (FR, 1), 0) + t * FR

        def out_step(j, carry):
            cols = chunk(j, 256)
            rows = ctx_v[...].reshape(CL * FR, D)
            mixed = mm(rows, wout_v[:, cols]).reshape(CL, FR, 256) + audio_v[:, :, cols].astype(F32)
            mixed = mixed.astype(BF)
            mixed_v[:, :, cols] = mixed
            wide = mixed.astype(F32)
            for c in range(CL):
                kept = jnp.where(frame < lengths[c], wide[c], 0.0)
                fs_all[t, c:c + 1, cols] = jnp.sum(kept, axis=0, keepdims=True)
            return carry

        lax.fori_loop(0, 3, out_step, 0)

        f_copies = [
            remote(fs_all.at[t], fs_all.at[t], f_s.at[k], f_r.at[k], t_peer(k))
            for k in range(1, NT)
        ]
        for copy in f_copies:
            copy.start()

        ld_ve.wait()
        for copy in z_copies:
            copy.wait()
        pools = jnp.concatenate(
            [jnp.sum(zp[n:n + NT].astype(F32), axis=0) for n in (0, NT)], axis=0
        ).astype(BF)
        u = mm(pools, wve_v[...])
        embed = u / jnp.sqrt(jnp.sum(u * u, axis=1, keepdims=True) + 1e-06)
        gath[co, x, y] = embed.astype(BF)
        around = [0]
        for k in range(1, ny // 2 + 1):
            around += [k] if 2 * k == ny else [k, ny - k]
        y_copies = {
            k: remote(gath.at[co, x, y], gath.at[co, x, y], y_s.at[k], y_r.at[k], y_peer(k))
            for k in around[1:]
        }

        for k in around[1:]:
            y_copies[k].start()
        ve_v[...] = jnp.where(zh == 0, embed[:CL], embed[CL:])

        ld_ae.wait()
        for copy in f_copies:
            copy.wait()
        row4 = lax.broadcasted_iota(jnp.int32, (CL, 1), 0)
        count = jnp.zeros((CL, 1), F32)
        for c in range(CL):
            count = jnp.where(row4 == c, lengths[c].astype(F32), count)
        pool = jnp.sum(fs_all[...], axis=0) / count
        u = mm(jnp.concatenate([pool, pool], axis=0).astype(BF), wae_v[...])
        a_embed = u / jnp.sqrt(jnp.sum(u * u, axis=1, keepdims=True) + 1e-06)
        ae_v[...] = a_embed[:CL]

        for k in around[1:]:
            y_copies[k].wait_recv()
        step = 1 - 2 * co
        behind = (x + NX - step) % NX

        def to_core(n, xx):
            copy = remote(gath.at[co, xx], gath.at[co, xx], c_s.at[n], c_r.at[n], core_peer)
            copy.start()
            return copy

        block, ahead = gath.at[co, x], gath.at[co, behind]
        x_copies = [
            remote(block, block, x_s.at[0], x_r.at[0], x_peer(1)),
            remote(block, block, x_s.at[1], x_r.at[1], x_peer(NX - 1)),
            remote(ahead, ahead, x_s.at[2], x_r.at[2], (batch_of(y, (x + NX + step) % NX, zh, co), t)),
        ]
        x_copies[0].start()
        x_copies[1].start()
        c_copies = [to_core(0, x)]
        x_copies[0].wait_recv()
        x_copies[1].wait_recv()
        x_copies[2].start()
        c_copies.append(to_core(1, (x + NX - 1) % NX))
        c_copies.append(to_core(2, (x + 1) % NX))
        x_copies[2].wait_recv()
        c_copies.append(to_core(3, (x + 2) % NX))
        first = lax.broadcasted_iota(jnp.int32, (8, D), 0) < 4

        for n, xx in enumerate((x, (x + NX - 1) % NX, (x + 1) % NX, (x + 2) % NX)):
            c_copies[n].wait()

            def order_rows(yy, carry, xx=xx):
                one = gath[0, xx, yy].astype(F32)
                two = gath[1, xx, yy].astype(F32)
                top = jnp.where(first, one, pltpu.roll(two, 4, 0))
                bottom = jnp.where(first, pltpu.roll(one, 4, 0), two)
                gp[chunk(yy * NX + xx, 16), :] = jnp.concatenate([top, bottom], axis=0).astype(BF)
                return carry

            lax.fori_loop(0, ny, order_rows, 0)
        logits = mmt(a_embed.astype(BF), gp[...])[:CL] * 10.0 - 10.0
        lg_v[...] = logits
        ids = jnp.zeros((CL, 1), jnp.int32)
        for c in range(CL):
            ids = jnp.where(row4 == c, pair_ids[c], ids)
        column = lax.broadcasted_iota(jnp.int32, (CL, clips_all), 1)
        signed = jnp.where(column == ids, -logits, logits)
        loss = jnp.maximum(signed, 0.0) + jnp.log1p(jnp.exp(-jnp.abs(signed)))
        loss_v[...] = jnp.broadcast_to(jnp.sum(loss, axis=1, keepdims=True), (CL, 128))

        @pl.when(t < NT - 1)
        def _():
            up.wait_send()

        @pl.when(t > 0)
        def _():
            down.wait_send()

        for k in around[1:]:
            y_copies[k].wait_send()
        for copy in x_copies:
            copy.wait_send()

    return kernel


def solution(mesh):
    nb = mesh.shape["batch"]
    ny = nb // (NX * NZ * NC)
    clips_all = nb * CL

    def per_device(
        audio, video, pair_ids, windows, lengths, w_qkv, w_out, w_query, w_audio_embed, w_video_embed
    ):
        smem = pl.BlockSpec(memory_space=pltpu.SMEM)
        hbm = pl.BlockSpec(memory_space=pl.ANY)
        dma = pltpu.SemaphoreType.DMA
        vm = pltpu.VMEM
        held = (
            jax.ShapeDtypeStruct((CL, FR, D), BF),
            jax.ShapeDtypeStruct((CL, D), F32),
            jax.ShapeDtypeStruct((CL, D), F32),
            jax.ShapeDtypeStruct((CL, clips_all), F32),
            jax.ShapeDtypeStruct((CL, 128), F32),
        )
        parts = pl.pallas_call(
            make_kernel(ny),
            name="av_step",
            out_shape=tuple(vm(leaf.shape, leaf.dtype) for leaf in held),
            in_specs=[smem] * 3 + [hbm] * 7,
            out_specs=(pl.BlockSpec(memory_space=vm),) * 5,
            scratch_shapes=[
                vm((CL, FR, D), BF), vm((CL, VT, DV), BF),
                vm((D, D), BF), vm((D, D), BF), vm((D, D), BF), vm((D, D), BF),
                vm((DV, D), BF), vm((D, D), BF), vm((D, D), BF),
                vm((CL, 2 * HALO, D), BF), vm((CL, EXT, D), BF), vm((CL, EXT, D), BF),
                vm((CL, FR, D), BF), vm((CL, VT, D), BF), vm((CL * PAIRS, VT, 256), BF), vm((CL * PAIRS, VT, 128), BF),
                vm((CL, 128, 128), F32), vm((CL, 128, 128), F32),
                vm((48, 128), F32), vm((48, 128), F32),
                vm((CL, FR, D), BF),
                vm((NT, 48, 128), F32), vm((NT, CL, D), F32), vm((CL, D), F32), vm((NZ * NT, CL, D), BF),
                vm((NC, NX, ny, 8, D), BF), vm((clips_all, D), BF),
                dma((9,)), dma((2,)), dma((2,)),
                dma((NT,)), dma((NT,)), dma((NT,)), dma((NT,)),
                dma((NZ * NT,)), dma((NZ * NT,)),
                dma((ny,)), dma((ny,)), dma((3,)), dma((3,)), dma((NX,)), dma((NX,)),
            ],
            compiler_params=pltpu.CompilerParams(
                collective_id=0, has_side_effects=True, vmem_limit_bytes=56 * 1024 * 1024,
            ),
        )(windows, lengths, pair_ids, audio, video, w_qkv, w_out, w_query, w_audio_embed, w_video_embed)
        return pl.pallas_call(
            write_out,
            name="write_out",
            out_shape=held[:4] + (jax.ShapeDtypeStruct((CL,), F32),),
            in_specs=[pl.BlockSpec(memory_space=vm)] * 5,
            out_specs=(hbm,) * 4 + (smem,),
            scratch_shapes=[dma((4,))],
            compiler_params=pltpu.CompilerParams(vmem_limit_bytes=4 * 1024 * 1024),
        )(*parts)

    in_specs = (
        P("batch", "tm", None), P("batch", None, None), P("batch"), P("batch"), P("batch"),
        P(), P(), P(), P(), P(),
    )
    out_specs = (
        P("batch", "tm", None), P("batch", None), P("batch", None), P("batch", None), P("batch"),
    )
    return jax.shard_map(
        per_device, mesh=mesh, in_specs=in_specs, out_specs=out_specs, check_vma=False
    )
```

```python
import jax
import jax.numpy as jnp
from jax import lax
from jax.experimental import pallas as pl
from jax.experimental.pallas import tpu as pltpu
from jax.sharding import PartitionSpec as P

NEG = -1e30
BF = jnp.bfloat16
F32 = jnp.float32
MESH = pl.DeviceIdType.MESH

CL = 4
FR = 128
D = 768
VT = 128
DV = 1024
PAIRS = 6
HALO = 32
EXT = FR + 2 * HALO
NX = 4
NZ = 2
NC = 2
NT = 6


def mm(a, b):
    return jnp.dot(a, b, preferred_element_type=F32)


def mmt(a, b):
    return lax.dot_general(a, b, (((1,), (1,)), ((), ())), preferred_element_type=F32)


def chunk(j, size):
    return pl.ds(pl.multiple_of(j * size, size), size)


def write_out(mixed_v, ae_v, ve_v, lg_v, loss_v, mixed_o, ae_o, ve_o, lg_o, loss_o, sem):
    copies = [
        pltpu.make_async_copy(src, dst, sem.at[k])
        for k, (src, dst) in enumerate(
            ((mixed_v, mixed_o), (ae_v, ae_o), (ve_v, ve_o), (lg_v, lg_o))
        )
    ]
    for copy in copies:
        copy.start()
    for c in range(CL):
        loss_o[c] = jnp.max(loss_v[c:c + 1, :])
    for copy in copies:
        copy.wait()


def make_kernel(ny):
    clips_all = ny * NX * NZ * NC * CL

    def kernel(
        windows, lengths, pair_ids,
        audio_h, video_h, wqkv_h, wout_h, wask_h, wae_h, wve_h,
        mixed_v, ae_v, ve_v, lg_v, loss_v,
        audio_v, video_v, wq_v, wk_v, wv_v, wout_v, wask_v, wae_v, wve_v,
        hx, kx, vx, q_v, ask_v, e_v, o2_v, mt_v, lt_v, m_v, c_v, ctx_v,
        lse_all, fs_all, share, zp, gath, gp, blocks, both_a, sums, other,
        load_sem, halo_s, halo_r, l_s, l_r, f_s, f_r, z_s, z_r,
        y_s, y_r, w_s, w_r, x_s, x_r, a_s, a_r, p_s, p_r,
    ):
        b = lax.axis_index("batch")
        t = lax.axis_index("tm")
        co = b % NC
        zh = (b // NC) % NZ
        x = (b // (NC * NZ)) % NX
        y = b // (NC * NZ * NX)
        z = zh * NT + t

        def batch_of(yy, xx, zz, cc):
            return ((yy * NX + xx) * NZ + zz) * NC + cc

        def load(src, dst, k):
            return pltpu.make_async_copy(src, dst, load_sem.at[k])

        ld_audio = load(audio_h, audio_v, 0)
        ld_k = load(wqkv_h.at[:, pl.ds(D, D)], wk_v, 1)
        ld_v = load(wqkv_h.at[:, pl.ds(2 * D, D)], wv_v, 2)
        ld_video = load(video_h, video_v, 3)
        ld_ask = load(wask_h, wask_v, 4)
        ld_q = load(wqkv_h.at[:, pl.ds(0, D)], wq_v, 5)
        ld_out = load(wout_h, wout_v, 6)
        ld_ve = load(wve_h, wve_v, 7)
        ld_ae = load(wae_h, wae_v, 8)
        for copy in (ld_audio, ld_k, ld_video, ld_ask):
            copy.start()
        def z_peer(k):
            zz = (z + k) % (NZ * NT)
            return (batch_of(y, x, zz // NT, co), zz % NT)

        def t_peer(k):
            return (b, (t + k) % NT)

        def y_peer(k):
            return (batch_of((y + k) % ny, x, zh, co), t)

        def x_peer(k):
            return (batch_of(y, (x + k) % NX, zh, co), t)

        core_peer = (batch_of(y, x, zh, 1 - co), t)

        def y_cross(k):
            return (batch_of((y + k) % ny, x, zh, 1 - co), t)

        def trio(k, other):
            tt = (t // 3) * 3 + (t % 3 + k) % 3
            return (batch_of(y, x, zh, 1 - co if other else co), tt)

        far_y = sorted(range(1, ny), key=lambda k: -min(k, ny - k))
        far_z = sorted(range(1, NZ * NT), key=lambda k: -min(k, NZ * NT - k))

        peers = [z_peer(k) for k in range(1, NZ * NT)]
        peers += [y_peer(k) for k in range(1, ny)]
        peers += [x_peer(k) for k in range(1, NX)]
        peers += [core_peer]
        peers += [y_cross(k) for k in range(1, ny)]
        peers += [trio(k, True) for k in (1, 2)]
        barrier = pltpu.get_barrier_semaphore()
        for peer in peers:
            pl.semaphore_signal(barrier, inc=1, device_id=peer, device_id_type=MESH)

        def remote(src, dst, s, r, peer):
            return pltpu.make_async_remote_copy(
                src_ref=src, dst_ref=dst, send_sem=s, recv_sem=r,
                device_id=peer, device_id_type=MESH,
            )

        def project(j, weight, dst):
            cols = chunk(j, 256)
            rows = audio_v[...].reshape(CL * FR, D)
            dst[:, HALO:HALO + FR, cols] = mm(rows, weight[:, cols]).astype(BF).reshape(CL, FR, 256)

        def k_step(j, carry):
            project(j, wk_v, kx)
            return carry

        def v_step(j, carry):
            project(j, wv_v, vx)
            return carry

        def q_step(j, carry):
            cols = chunk(j, 256)
            rows = audio_v[...].reshape(CL * FR, D)
            q = mm(rows, wq_v[:, cols]).astype(BF) * jnp.asarray(0.125, BF)
            q_v[:, :, cols] = q.reshape(CL, FR, 256)
            return carry

        def ask_step(j, carry):
            cols = chunk(j, 256)
            rows = video_v[...].reshape(CL * VT, DV)
            ask = mm(rows, wask_v[:, cols]).astype(BF) * jnp.asarray(0.125, BF)
            ask_v[:, :, cols] = ask.reshape(CL, VT, 256)
            return carry

        ld_audio.wait()
        ld_k.wait()
        lax.fori_loop(0, 3, k_step, 0)
        ld_video.wait()
        ld_ask.wait()
        for copy in (ld_v, ld_q, ld_ve, ld_out, ld_ae):
            copy.start()
        lax.fori_loop(0, 3, ask_step, 0)

        lane = lax.broadcasted_iota(jnp.int32, (128, 128), 1)
        low = lane < 64
        lane_row = lax.broadcasted_iota(jnp.int32, (1, 128), 1)
        zero_b = jnp.zeros((128, 128), BF)

        def split_heads(block):
            return jnp.concatenate(
                [jnp.where(low, block, zero_b), jnp.where(low, zero_b, block)], axis=0
            )

        marks = jnp.concatenate(
            [jnp.where(low, 1.0, 0.0), jnp.where(low, 0.0, 1.0)], axis=0
        ).astype(BF)

        def cross_clip(c, carry):
            key_bias = jnp.where(t * FR + lane_row < lengths[c], 0.0, NEG)
            peak = jnp.zeros((128, 128), F32)
            total = jnp.zeros((128, 128), F32)
            pairs = [slice(128 * p, 128 * p + 128) for p in range(PAIRS)]
            scores = [
                mmt(ask_v[c, :, cols], split_heads(kx[c, HALO:HALO + FR, cols])) for cols in pairs
            ]
            for p in range(PAIRS):
                here = (lane & 63) == p
                tops, es = [], []
                for h in range(2):
                    part = scores[p][:, 128 * h:128 * h + 128] + key_bias
                    m = jnp.max(part, axis=1, keepdims=True)
                    tops.append(m)
                    es.append(jnp.exp(part - m).astype(BF))
                e = jnp.concatenate(es, axis=1)
                e_v[c * PAIRS + p] = e
                peak = jnp.where(here, jnp.where(low, tops[0], tops[1]), peak)
                total = jnp.where(here, mm(e, marks), total)
            mt_v[c] = peak
            lt_v[c] = total
            return carry

        lax.fori_loop(0, CL, cross_clip, 0)

        def table(ref):
            acc = ref[0]
            for c in range(1, CL):
                acc = acc + pltpu.roll(ref[c], PAIRS * c, 1)
            flat = jnp.transpose(acc)
            return jnp.concatenate([flat[0:24], flat[64:88]], axis=0)

        peak48 = table(mt_v)
        m_v[...] = peak48
        lse_all[t] = peak48 + jnp.log(table(lt_v))

        pl.semaphore_wait(barrier, len(peers))

        up = remote(
            audio_v.at[:, pl.ds(FR - HALO, HALO), :], hx.at[:, pl.ds(0, HALO), :],
            halo_s.at[0], halo_r.at[0], (b, jnp.minimum(t + 1, NT - 1)),
        )
        down = remote(
            audio_v.at[:, pl.ds(0, HALO), :], hx.at[:, pl.ds(HALO, HALO), :],
            halo_s.at[1], halo_r.at[1], (b, jnp.maximum(t - 1, 0)),
        )

        l_copies = [
            remote(lse_all.at[t], lse_all.at[t], l_s.at[k], l_r.at[k], t_peer(k))
            for k in range(1, NT)
        ]
        for copy in l_copies:
            copy.start()

        @pl.when(t < NT - 1)
        def _():
            up.start()

        @pl.when(t > 0)
        def _():
            down.start()

        @pl.when(t == 0)
        def _():
            hx[:, 0:HALO, :] = jnp.zeros((CL, HALO, D), BF)

        @pl.when(t == NT - 1)
        def _():
            hx[:, HALO:2 * HALO, :] = jnp.zeros((CL, HALO, D), BF)

        ld_v.wait()
        lax.fori_loop(0, 3, v_step, 0)

        def hear_clip(c, carry):
            for p in range(PAIRS):
                cols = slice(128 * p, 128 * p + 128)
                heard = mm(e_v[c * PAIRS + p], split_heads(vx[c, HALO:HALO + FR, cols]))
                o2_v[c * PAIRS + p] = heard.astype(BF)
            return carry

        lax.fori_loop(0, CL, hear_clip, 0)

        ld_q.wait()
        lax.fori_loop(0, 3, q_step, 0)

        for copy in l_copies:
            copy.wait()
        lse = lse_all[...]
        highest = jnp.max(lse, axis=0)
        whole = highest + jnp.log(jnp.sum(jnp.exp(lse - highest[None]), axis=0))
        c_v[...] = jnp.exp(m_v[...] - whole) * (1.0 / VT)
        for c in range(CL):
            for p in range(PAIRS):
                r = c * PAIRS + p
                pair = jnp.concatenate([c_v[r:r + 1], c_v[24 + r:25 + r]], axis=0).astype(BF)
                both = mm(pair, o2_v[r])
                share[c:c + 1, 128 * p:128 * p + 128] = jnp.where(
                    lane_row < 64, both[0:1], both[1:2]
                )

        zp[z] = share[...].astype(BF)
        z_copies = [
            remote(zp.at[z], zp.at[z], z_s.at[k], z_r.at[k], z_peer(k))
            for k in far_z
        ]
        for copy in z_copies:
            copy.start()

        @pl.when(t > 0)
        def _():
            up.wait_recv()

        @pl.when(t < NT - 1)
        def _():
            down.wait_recv()

        def halo_step(j, carry):
            cols = chunk(j, 256)
            rows = hx[...].reshape(CL * 2 * HALO, D)
            k = mm(rows, wk_v[:, cols]).astype(BF).reshape(CL, 2 * HALO, 256)
            kx[:, 0:HALO, cols] = k[:, :HALO]
            kx[:, HALO + FR:EXT, cols] = k[:, HALO:]
            v = mm(rows, wv_v[:, cols]).astype(BF).reshape(CL, 2 * HALO, 256)
            vx[:, 0:HALO, cols] = v[:, :HALO]
            vx[:, HALO + FR:EXT, cols] = v[:, HALO:]
            return carry

        lax.fori_loop(0, 3, halo_step, 0)

        row64 = lax.broadcasted_iota(jnp.int32, (64, 128), 0)
        lane64 = lax.broadcasted_iota(jnp.int32, (64, 128), 1)
        offset = row64 + HALO - lane64
        distance = jnp.abs(offset)

        def window_clip(c, carry):
            near = distance <= windows[c]
            length = lengths[c]
            biases = []
            for i in range(2):
                key_pos = lane64 + (t * FR + 64 * i - HALO)
                allowed = near & (key_pos >= 0) & ((key_pos < length) | (offset == 0))
                biases.append(jnp.where(allowed, 0.0, NEG))
            blocks = [
                (i, slice(64 * i, 64 * i + 64), slice(64 * i, 64 * i + 128), slice(128 * p, 128 * p + 128))
                for i in range(2) for p in range(PAIRS)
            ]
            scores = [
                mmt(q_v[c, rows, cols], split_heads(kx[c, keys, cols])) for _, rows, keys, cols in blocks
            ]
            weights = []
            for (i, _, _, _), s in zip(blocks, scores):
                es = []
                for h in range(2):
                    part = s[:, 128 * h:128 * h + 128] + biases[i]
                    m = jnp.max(part, axis=1, keepdims=True)
                    es.append(jnp.exp(part - m).astype(BF))
                weights.append(jnp.concatenate(es, axis=1))
            for (_, rows, keys, cols), e in zip(blocks, weights):
                values = split_heads(vx[c, keys, cols])
                o = mm(e, jnp.concatenate([values, marks], axis=1))
                ctx_v[c, rows, cols] = (o[:, :128] / o[:, 128:]).astype(BF)
            return carry

        lax.fori_loop(0, CL, window_clip, 0)

        ld_out.wait()
        frame = lax.broadcasted_iota(jnp.int32, (FR, 1), 0) + t * FR

        def out_step(j, carry):
            cols = chunk(j, 256)
            rows = ctx_v[...].reshape(CL * FR, D)
            mixed = mm(rows, wout_v[:, cols]).reshape(CL, FR, 256) + audio_v[:, :, cols].astype(F32)
            mixed = mixed.astype(BF)
            mixed_v[:, :, cols] = mixed
            wide = mixed.astype(F32)
            for c in range(CL):
                kept = jnp.where(frame < lengths[c], wide[c], 0.0)
                fs_all[t, c:c + 1, cols] = jnp.sum(kept, axis=0, keepdims=True)
            return carry

        lax.fori_loop(0, 3, out_step, 0)

        f_copies = [
            remote(fs_all.at[t], fs_all.at[t], f_s.at[k], f_r.at[k], t_peer(k))
            for k in range(1, NT)
        ]
        for copy in f_copies:
            copy.start()

        ld_ve.wait()
        for copy in z_copies:
            copy.wait()
        pools = jnp.concatenate(
            [jnp.sum(zp[n:n + NT].astype(F32), axis=0) for n in (0, NT)], axis=0
        ).astype(BF)
        u = mm(pools, wve_v[...])
        embed = u / jnp.sqrt(jnp.sum(u * u, axis=1, keepdims=True) + 1e-06)
        mine = (t % 3) * 2 + co
        theirs = (t % 3) * 2 + 1 - co
        for p in range(PAIRS):
            blocks[p] = embed[:, 128 * p:128 * p + 128].astype(BF)
        gath[x, y, co] = blocks[mine]
        y_copies = [
            remote(blocks.at[theirs], gath.at[x, y, co], w_s.at[k], w_r.at[k], y_cross(k))
            for k in far_y + [0]
        ]
        y_copies += [
            remote(blocks.at[mine], gath.at[x, y, co], y_s.at[k], y_r.at[k], y_peer(k))
            for k in far_y
        ]
        for copy in y_copies:
            copy.start()
        ve_v[...] = jnp.where(zh == 0, embed[:CL], embed[CL:])

        ld_ae.wait()
        for copy in f_copies:
            copy.wait()
        row4 = lax.broadcasted_iota(jnp.int32, (CL, 1), 0)
        count = jnp.zeros((CL, 1), F32)
        for c in range(CL):
            count = jnp.where(row4 == c, lengths[c].astype(F32), count)
        pool = jnp.sum(fs_all[...], axis=0) / count
        u = mm(jnp.concatenate([pool, pool], axis=0).astype(BF), wae_v[...])
        a_embed = u / jnp.sqrt(jnp.sum(u * u, axis=1, keepdims=True) + 1e-06)
        ae_v[...] = a_embed[:CL]
        both_a[co] = a_embed[:CL]
        a_copy = remote(both_a.at[co], both_a.at[co], a_s, a_r, core_peer)
        a_copy.start()

        for copy in y_copies:
            copy.wait()
        x_copies = [
            remote(gath.at[x], gath.at[x], x_s.at[k], x_r.at[k], x_peer(k)) for k in (2, 1, 3)
        ]
        for copy in x_copies:
            copy.start()
        first = lax.broadcasted_iota(jnp.int32, (8, 128), 0) < 4

        def order(xx):
            def order_rows(yy, carry):
                one = gath[xx, yy, 0].astype(F32)
                two = gath[xx, yy, 1].astype(F32)
                top = jnp.where(first, one, pltpu.roll(two, 4, 0))
                bottom = jnp.where(first, pltpu.roll(one, 4, 0), two)
                gp[chunk(yy * NX + xx, 16), :] = jnp.concatenate([top, bottom], axis=0).astype(BF)
                return carry

            lax.fori_loop(0, ny, order_rows, 0, unroll=True)

        order(x)
        a_copy.wait()
        for copy in x_copies:
            copy.wait()
        for k in range(1, NX):
            order((x + k) % NX)

        cols = pl.ds(pl.multiple_of(mine * 128, 128), 128)
        a8 = jnp.concatenate([both_a[0, :, cols], both_a[1, :, cols]], axis=0).astype(BF)
        partial = mmt(a8, gp[...])
        sums[mine] = jnp.where(co == 0, partial[:CL], partial[CL:])
        other[...] = jnp.where(co == 0, partial[CL:], partial[:CL])
        p_copies = [
            remote(other, sums.at[mine], p_s.at[k], p_r.at[k], trio(k, True)) for k in range(3)
        ]
        p_copies += [
            remote(sums.at[mine], sums.at[mine], p_s.at[2 + k], p_r.at[2 + k], trio(k, False))
            for k in (1, 2)
        ]
        for copy in p_copies:
            copy.start()
        for copy in p_copies:
            copy.wait()
        logits = jnp.sum(sums[...], axis=0) * 10.0 - 10.0
        lg_v[...] = logits
        ids = jnp.zeros((CL, 1), jnp.int32)
        for c in range(CL):
            ids = jnp.where(row4 == c, pair_ids[c], ids)
        column = lax.broadcasted_iota(jnp.int32, (CL, clips_all), 1)
        signed = jnp.where(column == ids, -logits, logits)
        loss = jnp.maximum(signed, 0.0) + jnp.log1p(jnp.exp(-jnp.abs(signed)))
        loss_v[...] = jnp.broadcast_to(jnp.sum(loss, axis=1, keepdims=True), (CL, 128))

        @pl.when(t < NT - 1)
        def _():
            up.wait_send()

        @pl.when(t > 0)
        def _():
            down.wait_send()

    return kernel


def solution(mesh):
    nb = mesh.shape["batch"]
    ny = nb // (NX * NZ * NC)
    clips_all = nb * CL

    def per_device(
        audio, video, pair_ids, windows, lengths, w_qkv, w_out, w_query, w_audio_embed, w_video_embed
    ):
        smem = pl.BlockSpec(memory_space=pltpu.SMEM)
        hbm = pl.BlockSpec(memory_space=pl.ANY)
        dma = pltpu.SemaphoreType.DMA
        vm = pltpu.VMEM
        held = (
            jax.ShapeDtypeStruct((CL, FR, D), BF),
            jax.ShapeDtypeStruct((CL, D), F32),
            jax.ShapeDtypeStruct((CL, D), F32),
            jax.ShapeDtypeStruct((CL, clips_all), F32),
            jax.ShapeDtypeStruct((CL, 128), F32),
        )
        parts = pl.pallas_call(
            make_kernel(ny),
            name="av_step",
            out_shape=tuple(vm(leaf.shape, leaf.dtype) for leaf in held),
            in_specs=[smem] * 3 + [hbm] * 7,
            out_specs=(pl.BlockSpec(memory_space=vm),) * 5,
            scratch_shapes=[
                vm((CL, FR, D), BF), vm((CL, VT, DV), BF),
                vm((D, D), BF), vm((D, D), BF), vm((D, D), BF), vm((D, D), BF),
                vm((DV, D), BF), vm((D, D), BF), vm((D, D), BF),
                vm((CL, 2 * HALO, D), BF), vm((CL, EXT, D), BF), vm((CL, EXT, D), BF),
                vm((CL, FR, D), BF), vm((CL, VT, D), BF), vm((CL * PAIRS, VT, 256), BF), vm((CL * PAIRS, VT, 128), BF),
                vm((CL, 128, 128), F32), vm((CL, 128, 128), F32),
                vm((48, 128), F32), vm((48, 128), F32),
                vm((CL, FR, D), BF),
                vm((NT, 48, 128), F32), vm((NT, CL, D), F32), vm((CL, D), F32), vm((NZ * NT, CL, D), BF),
                vm((NX, ny, NC, 8, 128), BF), vm((clips_all, 128), BF),
                vm((PAIRS, 8, 128), BF), vm((NC, CL, D), F32),
                vm((6, CL, clips_all), F32), vm((CL, clips_all), F32),
                dma((9,)), dma((2,)), dma((2,)),
                dma((NT,)), dma((NT,)), dma((NT,)), dma((NT,)),
                dma((NZ * NT,)), dma((NZ * NT,)),
                dma((ny,)), dma((ny,)), dma((ny,)), dma((ny,)), dma((NX,)), dma((NX,)), dma, dma, dma((5,)), dma((5,)),
            ],
            compiler_params=pltpu.CompilerParams(
                collective_id=0, has_side_effects=True, vmem_limit_bytes=56 * 1024 * 1024,
            ),
        )(windows, lengths, pair_ids, audio, video, w_qkv, w_out, w_query, w_audio_embed, w_video_embed)
        return pl.pallas_call(
            write_out,
            name="write_out",
            out_shape=held[:4] + (jax.ShapeDtypeStruct((CL,), F32),),
            in_specs=[pl.BlockSpec(memory_space=vm)] * 5,
            out_specs=(hbm,) * 4 + (smem,),
            scratch_shapes=[dma((4,))],
            compiler_params=pltpu.CompilerParams(vmem_limit_bytes=4 * 1024 * 1024),
        )(*parts)

    in_specs = (
        P("batch", "tm", None), P("batch", None, None), P("batch"), P("batch"), P("batch"),
        P(), P(), P(), P(), P(),
    )
    out_specs = (
        P("batch", "tm", None), P("batch", None), P("batch", None), P("batch", None), P("batch"),
    )
    return jax.shard_map(
        per_device, mesh=mesh, in_specs=in_specs, out_specs=out_specs, check_vma=False
    )
```

```python
import jax
import jax.numpy as jnp
from jax import lax
from jax.experimental import pallas as pl
from jax.experimental.pallas import tpu as pltpu
from jax.sharding import PartitionSpec as P

NEG = -1e30
BF = jnp.bfloat16
F32 = jnp.float32
MESH = pl.DeviceIdType.MESH

CL = 4
FR = 128
D = 768
VT = 128
DV = 1024
PAIRS = 6
HALO = 32
EXT = FR + 2 * HALO
NX = 4
NZ = 2
NC = 2
NT = 6


def mm(a, b):
    return jnp.dot(a, b, preferred_element_type=F32)


def mmt(a, b):
    return lax.dot_general(a, b, (((1,), (1,)), ((), ())), preferred_element_type=F32)


def chunk(j, size):
    return pl.ds(pl.multiple_of(j * size, size), size)


def write_out(mixed_v, ae_v, ve_v, lg_v, loss_v, mixed_o, ae_o, ve_o, lg_o, loss_o, sem):
    copies = [
        pltpu.make_async_copy(src, dst, sem.at[k])
        for k, (src, dst) in enumerate(
            ((mixed_v, mixed_o), (ae_v, ae_o), (ve_v, ve_o), (lg_v, lg_o))
        )
    ]
    for copy in copies:
        copy.start()
    for c in range(CL):
        loss_o[c] = jnp.max(loss_v[c:c + 1, :])
    for copy in copies:
        copy.wait()


def make_kernel(ny):
    clips_all = ny * NX * NZ * NC * CL

    def kernel(
        windows, lengths, pair_ids,
        audio_h, video_h, wqkv_h, wout_h, wask_h, wae_h, wve_h,
        mixed_v, ae_v, ve_v, lg_v, loss_v,
        audio_v, video_v, wq_v, wk_v, wv_v, wout_v, wask_v, wae_v, wve_v,
        hx, kx, vx, q_v, ask_v, e_v, o2_v, mt_v, lt_v, m_v, ctx_v,
        lse_all, fs_all, share, zp, gath, gp, blocks, both_a, sums, other,
        load_sem, halo_s, halo_r, l_s, l_r, f_s, f_r, z_s, z_r,
        y_s, y_r, w_s, w_r, x_s, x_r, a_s, a_r, p_s, p_r,
    ):
        b = lax.axis_index("batch")
        t = lax.axis_index("tm")
        co = b % NC
        zh = (b // NC) % NZ
        x = (b // (NC * NZ)) % NX
        y = b // (NC * NZ * NX)
        z = zh * NT + t

        def batch_of(yy, xx, zz, cc):
            return ((yy * NX + xx) * NZ + zz) * NC + cc

        def load(src, dst, k):
            return pltpu.make_async_copy(src, dst, load_sem.at[k])

        ld_audio = load(audio_h, audio_v, 0)
        ld_k = load(wqkv_h.at[:, pl.ds(D, D)], wk_v, 1)
        ld_v = load(wqkv_h.at[:, pl.ds(2 * D, D)], wv_v, 2)
        ld_video = load(video_h, video_v, 3)
        ld_ask = load(wask_h, wask_v, 4)
        ld_q = load(wqkv_h.at[:, pl.ds(0, D)], wq_v, 5)
        ld_out = load(wout_h, wout_v, 6)
        ld_ve = load(wve_h, wve_v, 7)
        ld_ae = load(wae_h, wae_v, 8)
        for copy in (ld_audio, ld_k, ld_video, ld_ask):
            copy.start()
        def z_peer(k):
            zz = (z + k) % (NZ * NT)
            return (batch_of(y, x, zz // NT, co), zz % NT)

        def t_peer(k):
            return (b, (t + k) % NT)

        def y_peer(k):
            return (batch_of((y + k) % ny, x, zh, co), t)

        def x_peer(k):
            return (batch_of(y, (x + k) % NX, zh, co), t)

        core_peer = (batch_of(y, x, zh, 1 - co), t)

        def y_cross(k):
            return (batch_of((y + k) % ny, x, zh, 1 - co), t)

        def trio(k, other):
            tt = (t // 3) * 3 + (t % 3 + k) % 3
            return (batch_of(y, x, zh, 1 - co if other else co), tt)

        far_y = sorted(range(1, ny), key=lambda k: -min(k, ny - k))
        far_z = sorted(range(1, NZ * NT), key=lambda k: -min(k, NZ * NT - k))

        peers = [z_peer(k) for k in range(1, NZ * NT)]
        peers += [y_peer(k) for k in range(1, ny)]
        peers += [x_peer(k) for k in range(1, NX)]
        peers += [core_peer]
        peers += [y_cross(k) for k in range(1, ny)]
        peers += [trio(k, True) for k in (1, 2)]
        barrier = pltpu.get_barrier_semaphore()
        for peer in peers:
            pl.semaphore_signal(barrier, inc=1, device_id=peer, device_id_type=MESH)

        def remote(src, dst, s, r, peer):
            return pltpu.make_async_remote_copy(
                src_ref=src, dst_ref=dst, send_sem=s, recv_sem=r,
                device_id=peer, device_id_type=MESH,
            )

        def project(j, weight, dst):
            cols = chunk(j, 256)
            rows = audio_v[...].reshape(CL * FR, D)
            dst[:, HALO:HALO + FR, cols] = mm(rows, weight[:, cols]).astype(BF).reshape(CL, FR, 256)

        def k_step(j, carry):
            project(j, wk_v, kx)
            return carry

        def v_step(j, carry):
            project(j, wv_v, vx)
            return carry

        def q_step(j, carry):
            cols = chunk(j, 256)
            rows = audio_v[...].reshape(CL * FR, D)
            q = mm(rows, wq_v[:, cols]).astype(BF) * jnp.asarray(0.125, BF)
            q_v[:, :, cols] = q.reshape(CL, FR, 256)
            return carry

        def ask_step(j, carry):
            cols = chunk(j, 256)
            rows = video_v[...].reshape(CL * VT, DV)
            ask = mm(rows, wask_v[:, cols]).astype(BF) * jnp.asarray(0.125, BF)
            ask_v[:, :, cols] = ask.reshape(CL, VT, 256)
            return carry

        ld_audio.wait()
        ld_k.wait()
        lax.fori_loop(0, 3, k_step, 0)
        ld_video.wait()
        ld_ask.wait()
        for copy in (ld_v, ld_q, ld_ve, ld_out, ld_ae):
            copy.start()
        lax.fori_loop(0, 3, ask_step, 0)

        lane = lax.broadcasted_iota(jnp.int32, (128, 128), 1)
        low = lane < 64
        lane_row = lax.broadcasted_iota(jnp.int32, (1, 128), 1)
        zero_b = jnp.zeros((128, 128), BF)

        def split_heads(block):
            return jnp.concatenate(
                [jnp.where(low, block, zero_b), jnp.where(low, zero_b, block)], axis=0
            )

        marks = jnp.concatenate(
            [jnp.where(low, 1.0, 0.0), jnp.where(low, 0.0, 1.0)], axis=0
        ).astype(BF)

        def cross_clip(c, carry):
            key_bias = jnp.where(t * FR + lane_row < lengths[c], 0.0, NEG)
            peak = jnp.zeros((128, 128), F32)
            total = jnp.zeros((128, 128), F32)
            pairs = [slice(128 * p, 128 * p + 128) for p in range(PAIRS)]
            scores = [
                mmt(ask_v[c, :, cols], split_heads(kx[c, HALO:HALO + FR, cols])) for cols in pairs
            ]
            weights = []
            for p in range(PAIRS):
                tops, es = [], []
                for h in range(2):
                    part = scores[p][:, 128 * h:128 * h + 128] + key_bias
                    m = jnp.max(part, axis=1, keepdims=True)
                    tops.append(m)
                    es.append(jnp.exp(part - m).astype(BF))
                weights.append(jnp.concatenate(es, axis=1))
                e_v[c * PAIRS + p] = weights[p]
                peak = jnp.where((lane & 63) == p, jnp.where(low, tops[0], tops[1]), peak)
            sums_all = mm(jnp.concatenate(weights, axis=0), marks)
            for p in range(PAIRS):
                total = jnp.where((lane & 63) == p, sums_all[VT * p:VT * p + VT], total)
            mt_v[c] = peak
            lt_v[c] = total
            return carry

        lax.fori_loop(0, CL, cross_clip, 0)

        def table(ref):
            acc = ref[0]
            for c in range(1, CL):
                acc = acc + pltpu.roll(ref[c], PAIRS * c, 1)
            flat = jnp.transpose(acc)
            return jnp.concatenate([flat[0:24], flat[64:88]], axis=0)

        peak48 = table(mt_v)
        m_v[...] = peak48
        lse_all[t] = peak48 + jnp.log(table(lt_v))

        pl.semaphore_wait(barrier, len(peers))

        up = remote(
            audio_v.at[:, pl.ds(FR - HALO, HALO), :], hx.at[:, pl.ds(0, HALO), :],
            halo_s.at[0], halo_r.at[0], (b, jnp.minimum(t + 1, NT - 1)),
        )
        down = remote(
            audio_v.at[:, pl.ds(0, HALO), :], hx.at[:, pl.ds(HALO, HALO), :],
            halo_s.at[1], halo_r.at[1], (b, jnp.maximum(t - 1, 0)),
        )

        l_copies = [
            remote(lse_all.at[t], lse_all.at[t], l_s.at[k], l_r.at[k], t_peer(k))
            for k in range(1, NT)
        ]
        for copy in l_copies:
            copy.start()

        ld_v.wait()
        lax.fori_loop(0, 3, v_step, 0)

        def hear_clip(c, carry):
            for p in range(PAIRS):
                cols = slice(128 * p, 128 * p + 128)
                heard = mm(e_v[c * PAIRS + p], split_heads(vx[c, HALO:HALO + FR, cols]))
                o2_v[c, :, cols] = heard.astype(BF)
            return carry

        lax.fori_loop(0, CL, hear_clip, 0)

        ld_q.wait()
        lax.fori_loop(0, 3, q_step, 0)

        @pl.when(t < NT - 1)
        def _():
            up.start()

        @pl.when(t > 0)
        def _():
            down.start()

        @pl.when(t == 0)
        def _():
            hx[:, 0:HALO, :] = jnp.zeros((CL, HALO, D), BF)

        @pl.when(t == NT - 1)
        def _():
            hx[:, HALO:2 * HALO, :] = jnp.zeros((CL, HALO, D), BF)

        for copy in l_copies:
            copy.wait()
        lse = lse_all[...]
        highest = jnp.max(lse, axis=0)
        whole = highest + jnp.log(jnp.sum(jnp.exp(lse - highest[None]), axis=0))
        parts = (jnp.exp(m_v[...] - whole) * (1.0 / VT)).astype(BF)
        wide = lax.broadcasted_iota(jnp.int32, (48, D), 1)
        source = ((wide >> 6) & 1) * 24 + (wide >> 7) - lax.broadcasted_iota(jnp.int32, (48, D), 0)
        for c in range(CL):
            heard = mm(parts, o2_v[c])
            kept = jnp.where(source == -PAIRS * c, heard, 0.0)
            share[c:c + 1, :] = jnp.sum(kept, axis=0, keepdims=True)
        zp[z] = share[...].astype(BF)
        z_copies = [
            remote(zp.at[z], zp.at[z], z_s.at[k], z_r.at[k], z_peer(k))
            for k in far_z
        ]
        for copy in z_copies:
            copy.start()

        @pl.when(t > 0)
        def _():
            up.wait_recv()

        @pl.when(t < NT - 1)
        def _():
            down.wait_recv()

        def halo_step(j, carry):
            cols = chunk(j, 256)
            rows = hx[...].reshape(CL * 2 * HALO, D)
            k = mm(rows, wk_v[:, cols]).astype(BF).reshape(CL, 2 * HALO, 256)
            kx[:, 0:HALO, cols] = k[:, :HALO]
            kx[:, HALO + FR:EXT, cols] = k[:, HALO:]
            v = mm(rows, wv_v[:, cols]).astype(BF).reshape(CL, 2 * HALO, 256)
            vx[:, 0:HALO, cols] = v[:, :HALO]
            vx[:, HALO + FR:EXT, cols] = v[:, HALO:]
            return carry

        lax.fori_loop(0, 3, halo_step, 0)

        row64 = lax.broadcasted_iota(jnp.int32, (64, 128), 0)
        lane64 = lax.broadcasted_iota(jnp.int32, (64, 128), 1)
        offset = row64 + HALO - lane64
        distance = jnp.abs(offset)

        def window_clip(c, carry):
            near = distance <= windows[c]
            length = lengths[c]
            biases = []
            for i in range(2):
                key_pos = lane64 + (t * FR + 64 * i - HALO)
                allowed = near & (key_pos >= 0) & ((key_pos < length) | (offset == 0))
                biases.append(jnp.where(allowed, 0.0, NEG))
            blocks = [
                (i, slice(64 * i, 64 * i + 64), slice(64 * i, 64 * i + 128), slice(128 * p, 128 * p + 128))
                for i in range(2) for p in range(PAIRS)
            ]
            scores = [
                mmt(q_v[c, rows, cols], split_heads(kx[c, keys, cols])) for _, rows, keys, cols in blocks
            ]
            weights = []
            for (i, _, _, _), s in zip(blocks, scores):
                es = []
                for h in range(2):
                    part = s[:, 128 * h:128 * h + 128] + biases[i]
                    m = jnp.max(part, axis=1, keepdims=True)
                    es.append(jnp.exp(part - m).astype(BF))
                weights.append(jnp.concatenate(es, axis=1))
            for (_, rows, keys, cols), e in zip(blocks, weights):
                values = split_heads(vx[c, keys, cols])
                o = mm(e, jnp.concatenate([values, marks], axis=1))
                ctx_v[c, rows, cols] = (o[:, :128] / o[:, 128:]).astype(BF)
            return carry

        lax.fori_loop(0, CL, window_clip, 0)

        ld_ve.wait()
        for copy in z_copies:
            copy.wait()
        pools = jnp.concatenate(
            [jnp.sum(zp[n:n + NT].astype(F32), axis=0) for n in (0, NT)], axis=0
        ).astype(BF)
        u = mm(pools, wve_v[...])
        embed = u / jnp.sqrt(jnp.sum(u * u, axis=1, keepdims=True) + 1e-06)
        mine = (t % 3) * 2 + co
        theirs = (t % 3) * 2 + 1 - co
        for p in range(PAIRS):
            blocks[p] = embed[:, 128 * p:128 * p + 128].astype(BF)
        gath[x, y, co] = blocks[mine]
        y_copies = [
            remote(blocks.at[theirs], gath.at[x, y, co], w_s.at[k], w_r.at[k], y_cross(k))
            for k in far_y + [0]
        ]
        y_copies += [
            remote(blocks.at[mine], gath.at[x, y, co], y_s.at[k], y_r.at[k], y_peer(k))
            for k in far_y
        ]
        for copy in y_copies:
            copy.start()
        ve_v[...] = jnp.where(zh == 0, embed[:CL], embed[CL:])

        ld_out.wait()
        frame = lax.broadcasted_iota(jnp.int32, (FR, 1), 0) + t * FR

        def out_step(j, carry):
            cols = chunk(j, 256)
            rows = ctx_v[...].reshape(CL * FR, D)
            mixed = mm(rows, wout_v[:, cols]).reshape(CL, FR, 256) + audio_v[:, :, cols].astype(F32)
            mixed = mixed.astype(BF)
            mixed_v[:, :, cols] = mixed
            wide = mixed.astype(F32)
            for c in range(CL):
                kept = jnp.where(frame < lengths[c], wide[c], 0.0)
                fs_all[t, c:c + 1, cols] = jnp.sum(kept, axis=0, keepdims=True)
            return carry

        lax.fori_loop(0, 3, out_step, 0)

        f_copies = [
            remote(fs_all.at[t], fs_all.at[t], f_s.at[k], f_r.at[k], t_peer(k))
            for k in range(1, NT)
        ]
        for copy in f_copies:
            copy.start()

        for copy in y_copies:
            copy.wait()
        x_copies = [
            remote(gath.at[x], gath.at[x], x_s.at[k], x_r.at[k], x_peer(k)) for k in (2, 1, 3)
        ]
        for copy in x_copies:
            copy.start()

        ld_ae.wait()
        for copy in f_copies:
            copy.wait()
        row4 = lax.broadcasted_iota(jnp.int32, (CL, 1), 0)
        count = jnp.zeros((CL, 1), F32)
        for c in range(CL):
            count = jnp.where(row4 == c, lengths[c].astype(F32), count)
        pool = jnp.sum(fs_all[...], axis=0) / count
        u = mm(jnp.concatenate([pool, pool], axis=0).astype(BF), wae_v[...])
        a_embed = u / jnp.sqrt(jnp.sum(u * u, axis=1, keepdims=True) + 1e-06)
        ae_v[...] = a_embed[:CL]
        both_a[co] = a_embed[:CL]
        a_copy = remote(both_a.at[co], both_a.at[co], a_s, a_r, core_peer)
        a_copy.start()

        first = lax.broadcasted_iota(jnp.int32, (8, 128), 0) < 4

        def order(xx):
            def order_rows(yy, carry):
                one = gath[xx, yy, 0].astype(F32)
                two = gath[xx, yy, 1].astype(F32)
                top = jnp.where(first, one, pltpu.roll(two, 4, 0))
                bottom = jnp.where(first, pltpu.roll(one, 4, 0), two)
                gp[chunk(yy * NX + xx, 16), :] = jnp.concatenate([top, bottom], axis=0).astype(BF)
                return carry

            lax.fori_loop(0, ny, order_rows, 0, unroll=True)

        order(x)
        a_copy.wait()
        for copy in x_copies:
            copy.wait()
        for k in range(1, NX):
            order((x + k) % NX)

        cols = pl.ds(pl.multiple_of(mine * 128, 128), 128)
        a8 = jnp.concatenate([both_a[0, :, cols], both_a[1, :, cols]], axis=0).astype(BF)
        partial = mmt(a8, gp[...])
        sums[mine] = jnp.where(co == 0, partial[:CL], partial[CL:])
        other[...] = jnp.where(co == 0, partial[CL:], partial[:CL])
        p_copies = [
            remote(other, sums.at[mine], p_s.at[k], p_r.at[k], trio(k, True)) for k in range(3)
        ]
        p_copies += [
            remote(sums.at[mine], sums.at[mine], p_s.at[2 + k], p_r.at[2 + k], trio(k, False))
            for k in (1, 2)
        ]
        for copy in p_copies:
            copy.start()
        for copy in p_copies:
            copy.wait()
        logits = jnp.sum(sums[...], axis=0) * 10.0 - 10.0
        lg_v[...] = logits
        ids = jnp.zeros((CL, 1), jnp.int32)
        for c in range(CL):
            ids = jnp.where(row4 == c, pair_ids[c], ids)
        column = lax.broadcasted_iota(jnp.int32, (CL, clips_all), 1)
        signed = jnp.where(column == ids, -logits, logits)
        loss = jnp.maximum(signed, 0.0) + jnp.log1p(jnp.exp(-jnp.abs(signed)))
        loss_v[...] = jnp.broadcast_to(jnp.sum(loss, axis=1, keepdims=True), (CL, 128))

        @pl.when(t < NT - 1)
        def _():
            up.wait_send()

        @pl.when(t > 0)
        def _():
            down.wait_send()

    return kernel


def solution(mesh):
    nb = mesh.shape["batch"]
    ny = nb // (NX * NZ * NC)
    clips_all = nb * CL

    def per_device(
        audio, video, pair_ids, windows, lengths, w_qkv, w_out, w_query, w_audio_embed, w_video_embed
    ):
        smem = pl.BlockSpec(memory_space=pltpu.SMEM)
        hbm = pl.BlockSpec(memory_space=pl.ANY)
        dma = pltpu.SemaphoreType.DMA
        vm = pltpu.VMEM
        held = (
            jax.ShapeDtypeStruct((CL, FR, D), BF),
            jax.ShapeDtypeStruct((CL, D), F32),
            jax.ShapeDtypeStruct((CL, D), F32),
            jax.ShapeDtypeStruct((CL, clips_all), F32),
            jax.ShapeDtypeStruct((CL, 128), F32),
        )
        parts = pl.pallas_call(
            make_kernel(ny),
            name="av_step",
            out_shape=tuple(vm(leaf.shape, leaf.dtype) for leaf in held),
            in_specs=[smem] * 3 + [hbm] * 7,
            out_specs=(pl.BlockSpec(memory_space=vm),) * 5,
            scratch_shapes=[
                vm((CL, FR, D), BF), vm((CL, VT, DV), BF),
                vm((D, D), BF), vm((D, D), BF), vm((D, D), BF), vm((D, D), BF),
                vm((DV, D), BF), vm((D, D), BF), vm((D, D), BF),
                vm((CL, 2 * HALO, D), BF), vm((CL, EXT, D), BF), vm((CL, EXT, D), BF),
                vm((CL, FR, D), BF), vm((CL, VT, D), BF), vm((CL * PAIRS, VT, 256), BF), vm((CL, VT, D), BF),
                vm((CL, 128, 128), F32), vm((CL, 128, 128), F32),
                vm((48, 128), F32),
                vm((CL, FR, D), BF),
                vm((NT, 48, 128), F32), vm((NT, CL, D), F32), vm((CL, D), F32), vm((NZ * NT, CL, D), BF),
                vm((NX, ny, NC, 8, 128), BF), vm((clips_all, 128), BF),
                vm((PAIRS, 8, 128), BF), vm((NC, CL, D), F32),
                vm((6, CL, clips_all), F32), vm((CL, clips_all), F32),
                dma((9,)), dma((2,)), dma((2,)),
                dma((NT,)), dma((NT,)), dma((NT,)), dma((NT,)),
                dma((NZ * NT,)), dma((NZ * NT,)),
                dma((ny,)), dma((ny,)), dma((ny,)), dma((ny,)), dma((NX,)), dma((NX,)), dma, dma, dma((5,)), dma((5,)),
            ],
            compiler_params=pltpu.CompilerParams(
                collective_id=0, has_side_effects=True, vmem_limit_bytes=56 * 1024 * 1024,
            ),
        )(windows, lengths, pair_ids, audio, video, w_qkv, w_out, w_query, w_audio_embed, w_video_embed)
        return pl.pallas_call(
            write_out,
            name="write_out",
            out_shape=held[:4] + (jax.ShapeDtypeStruct((CL,), F32),),
            in_specs=[pl.BlockSpec(memory_space=vm)] * 5,
            out_specs=(hbm,) * 4 + (smem,),
            scratch_shapes=[dma((4,))],
            compiler_params=pltpu.CompilerParams(vmem_limit_bytes=4 * 1024 * 1024),
        )(*parts)

    in_specs = (
        P("batch", "tm", None), P("batch", None, None), P("batch"), P("batch"), P("batch"),
        P(), P(), P(), P(), P(),
    )
    out_specs = (
        P("batch", "tm", None), P("batch", None), P("batch", None), P("batch", None), P("batch"),
    )
    return jax.shard_map(
        per_device, mesh=mesh, in_specs=in_specs, out_specs=out_specs, check_vma=False
    )
```
